256 devices in a mesh: rows: 16 (over z_lo, y, core), tm: 16 (over x, z_hi).
Axes of the slice: x: 4, y: 4, z: 8 (z_hi: 4, z_lo: 2; z = z_hi * 2 + z_lo), core: 2. Of those that a mesh axis runs over, the one named last changes fastest.
Arguments:
- residual: float32 [64, 1024, 512], P('tm', 'rows'), may hold values from -45 to 45
- cycle_weight: float32 [64, 1024, 512], P('tm', 'rows'), may hold values from -0.75 to 0.75
- cycle_offsets: int32 [64, 2], replicated, may hold values from -6 to 6, as said below
Outputs:
- new_weight: float32 [64, 1024, 512], P('tm', 'rows')
- error: float32 [64, 1024, 512], P('tm', 'rows')
The draws below stay inside these ranges and needn't reach their ends.
Inputs may be any that keep to these rules, and one draw needn't show every extreme that they name: `cycle_offsets`: each row is a distinct (row, column) offset; together the rows are the 64 pixels (dy, dx) with 17 <= dy*dy + dx*dx <= 36, in an order drawn from the seed.
All inputs are finite; a program needn't handle non-finite values.
Results may differ from the reference program's by a relative error of at most 0.0003.
Values sent between devices are 32-bit elements; how exact they have to be, the bound alone decides.
A program may use at most 64 MiB of HBM per device.

```python
import jax
import jax.numpy as jnp
import numpy as np
from jax import lax

K = 64
COLS = 512
IMG_ROWS = 1024
FRAMES = 64


def cycle_table():
    points = []
    for row_off in range(-6, 7):
        for col_off in range(-6, 7):
            radius = row_off * row_off + col_off * col_off
            if radius >= 17 and radius <= 36:
                points.append((row_off, col_off))
    return np.array(points, dtype=np.int32)


def draw_cycle_offsets(key, part):
    table = jnp.asarray(cycle_table())
    order = jax.random.permutation(key, K)
    return table[order]


def draw_residual(key, part):
    key_base, key_frame, key_pixel = jax.random.split(key, 3)
    shape = (FRAMES, IMG_ROWS, COLS)
    base = jnp.clip(jax.random.normal(key_base, shape, jnp.float32), -6.0, 6.0)
    ramp = jnp.arange(FRAMES, dtype=jnp.float32) / max(FRAMES - 1, 1)
    frame_scale = 0.5 * jnp.exp(ramp * jnp.log(3.0)) * jnp.exp(jax.random.uniform(key_frame, (FRAMES,), jnp.float32, 0.0, jnp.log(3.3)))
    pixel_scale = jax.random.uniform(key_pixel, (IMG_ROWS, COLS), jnp.float32, 0.5, 1.5)
    return base * frame_scale[:, None, None] * pixel_scale[None]


def block_scale(stream_key, dims, shards, smallest, high):
    def one(dim, shards_of):
        heights = jax.random.uniform(jax.random.fold_in(jax.random.fold_in(stream_key, 6), dim), (shards_of,), jnp.float32, smallest / len(shards), high / len(shards))
        return jnp.repeat(jnp.exp(heights), dims[dim] // shards_of).reshape((-1,) + (1,) * (len(dims) - dim - 1))

    factor_of = one(*shards[0])
    for cut in shards[1:]:
        factor_of = factor_of * one(*cut)
    return factor_of


def bell_draw(key, dims, scale, most, cuts=(), held_as=jnp.bfloat16):
    values = jax.random.normal(key, dims, jnp.float32) * scale
    if len(cuts) > 0:
        values = block_scale(key, dims, cuts, -0.22, 0.18) * values
    return jnp.clip(values, min=-most, max=most).astype(held_as)


def setup_inputs(seed: int = 0) -> dict:
    splits = jax.random.split(jax.random.key(seed), 4)
    residual = draw_residual(jax.random.fold_in(splits[3], 71), 0)
    cycle_weight = bell_draw(splits[1], (K, IMG_ROWS, COLS), 0.125, 0.75, ((0, 16), (1, 16)), jnp.float32)
    cycle_offsets = draw_cycle_offsets(jax.random.fold_in(splits[3], 71), 0)
    return dict(residual=residual, cycle_weight=cycle_weight, cycle_offsets=cycle_offsets)


def shifted(padded, offset, frames, height, width):
    zero = jnp.zeros((), jnp.int32)
    return lax.dynamic_slice(padded, (zero, (offset[0] + 6).astype(jnp.int32), (offset[1] + 6).astype(jnp.int32)), (frames, height, width))


def reference(residual, cycle_weight, cycle_offsets):
    frames, height, width = residual.shape
    padded = jnp.pad(residual, ((0, 0), (6, 6), (6, 6)))

    def add_cycle(total, items):
        weight, offset = items
        return total + weight[None] * shifted(padded, offset, frames, height, width), None

    background, _ = lax.scan(add_cycle, jnp.zeros(residual.shape, jnp.float32), (cycle_weight, cycle_offsets))
    error = residual - background

    def grad_cycle(energy, offset):
        window = shifted(padded, offset, frames, height, width)
        return energy + jnp.sum(window * window, axis=0), jnp.sum(error * window, axis=0)

    energy, gradient = lax.scan(grad_cycle, jnp.zeros((height, width), jnp.float32), cycle_offsets)
    energy = energy / (K * FRAMES) + 1e-6
    new_weight = cycle_weight + gradient / (FRAMES * energy)[None]
    return new_weight, error
```

```python
import jax
import jax.numpy as jnp
import numpy as np
from jax import lax
from jax.sharding import PartitionSpec as P

HALO = 6


def with_halo(cells, sides, width):
    for axis, dim in sides:
        count = lax.axis_size(axis)
        ends = count - 1
        head = lax.slice_in_dim(cells, 0, width, axis=dim)
        tail = lax.slice_in_dim(cells, cells.shape[dim] - width, cells.shape[dim], axis=dim)
        cells = jnp.concatenate(
            [
                lax.ppermute(tail, axis, [(i, (i + 1) % count) for i in range(ends)]),
                cells,
                lax.ppermute(head, axis, [((i + 1) % count, i) for i in range(ends)]),
            ],
            axis=dim,
        )
    return cells


def cycle_points():
    points = []
    for row_off in range(-6, 7):
        for col_off in range(-6, 7):
            radius = row_off * row_off + col_off * col_off
            if radius >= 17 and radius <= 36:
                points.append((row_off, col_off))
    return points


def matching(cycle_offsets, points):
    table_rows = jnp.asarray(np.array([p[0] for p in points], dtype=np.int32))
    table_cols = jnp.asarray(np.array([p[1] for p in points], dtype=np.int32))
    same = (table_rows[:, None] == cycle_offsets[None, :, 0]) & (
        table_cols[:, None] == cycle_offsets[None, :, 1]
    )
    return same.astype(jnp.int32)


def tile_split(count, rows, cols):
    b = 1
    while b * 2 <= count and cols // (b * 2) >= 128 and count % (b * 2) == 0:
        b *= 2
    a = count // b
    return a, b


def tile_compute(rt, wt, order, place, points, h, w, frames_all, cycle):
    ordered_weight = jnp.take(wt, order, axis=0)
    background = jnp.zeros((rt.shape[0], h, w), jnp.float32)
    for index, (dy, dx) in enumerate(points):
        window = rt[:, HALO + dy : HALO + dy + h, HALO + dx : HALO + dx + w]
        background = background + ordered_weight[index][None] * window
    error = rt[:, HALO : HALO + h, HALO : HALO + w] - background
    grads = jnp.stack(
        [
            jnp.sum(error * rt[:, HALO + dy : HALO + dy + h, HALO + dx : HALO + dx + w], axis=0)
            for dy, dx in points
        ]
    )
    squares = jnp.sum(rt * rt, axis=0)
    energy_sum = jnp.zeros((h, w), jnp.float32)
    for dy, dx in points:
        energy_sum = energy_sum + squares[HALO + dy : HALO + dy + h, HALO + dx : HALO + dx + w]
    gradient = jnp.take(grads, place, axis=0)
    energy = energy_sum / (cycle * frames_all) + 1e-06
    new_weight = wt + gradient / (frames_all * energy)[None]
    return error, new_weight


def on_device(residual, cycle_weight, cycle_offsets):
    frames_dev, rows_dev, cols = residual.shape
    k_dev = cycle_weight.shape[0]
    cycle = cycle_offsets.shape[0]
    n = lax.axis_size("tm")
    frames_all = frames_dev * n
    points = cycle_points()
    same = matching(cycle_offsets, points)
    ks = jnp.arange(cycle, dtype=jnp.int32)
    order = jnp.sum(same * ks[None, :], axis=1)
    place = jnp.sum(same * ks[:, None], axis=0)

    a, b = tile_split(n, rows_dev, cols)
    h, w = rows_dev // a, cols // b

    extended = with_halo(residual, (("rows", 1),), HALO)
    padded = jnp.pad(extended, ((0, 0), (0, 0), (HALO, HALO)))
    res_tiles = jnp.stack(
        [
            padded[:, i * h : i * h + h + 2 * HALO, j * w : j * w + w + 2 * HALO]
            for i in range(a)
            for j in range(b)
        ]
    )
    rt = lax.all_to_all(res_tiles, "tm", 0, 0, tiled=True)
    rt = rt.reshape(frames_all, h + 2 * HALO, w + 2 * HALO)

    w_tiles = cycle_weight.reshape(k_dev, a, h, b, w).transpose(1, 3, 0, 2, 4)
    w_tiles = w_tiles.reshape(n, k_dev, h, w)
    wt = lax.all_to_all(w_tiles, "tm", 0, 0, tiled=True).reshape(cycle, h, w)

    error_t, new_t = tile_compute(rt, wt, order, place, points, h, w, frames_all, cycle)

    def back(x, lead):
        x = lax.all_to_all(x.reshape(n, lead, h, w), "tm", 0, 0, tiled=True)
        x = x.reshape(a, b, lead, h, w).transpose(2, 0, 3, 1, 4)
        return x.reshape(lead, rows_dev, cols)

    return back(new_t, k_dev), back(error_t, frames_dev)


def solution(mesh):
    in_specs = (P("tm", "rows", None), P("tm", "rows", None), P())
    out_specs = (P("tm", "rows", None), P("tm", "rows", None))
    return jax.shard_map(
        on_device, mesh=mesh, in_specs=in_specs, out_specs=out_specs, check_vma=False
    )
```

```python
import jax
import jax.numpy as jnp
import numpy as np
from jax import lax
from jax.sharding import PartitionSpec as P

HALO = 6


def with_halo(cells, sides, width):
    for axis, dim in sides:
        count = lax.axis_size(axis)
        ends = count - 1
        head = lax.slice_in_dim(cells, 0, width, axis=dim)
        tail = lax.slice_in_dim(cells, cells.shape[dim] - width, cells.shape[dim], axis=dim)
        cells = jnp.concatenate(
            [
                lax.ppermute(tail, axis, [(i, (i + 1) % count) for i in range(ends)]),
                cells,
                lax.ppermute(head, axis, [((i + 1) % count, i) for i in range(ends)]),
            ],
            axis=dim,
        )
    return cells


def cycle_points():
    points = []
    for row_off in range(-6, 7):
        for col_off in range(-6, 7):
            radius = row_off * row_off + col_off * col_off
            if radius >= 17 and radius <= 36:
                points.append((row_off, col_off))
    return points


def matching(cycle_offsets, points):
    table_rows = jnp.asarray(np.array([p[0] for p in points], dtype=np.int32))
    table_cols = jnp.asarray(np.array([p[1] for p in points], dtype=np.int32))
    same = (table_rows[:, None] == cycle_offsets[None, :, 0]) & (
        table_cols[:, None] == cycle_offsets[None, :, 1]
    )
    return same.astype(jnp.int32)


def tile_split(count, rows, cols):
    b = 1
    while b * 2 <= count and cols // (b * 2) >= 128 and count % (b * 2) == 0:
        b *= 2
    a = count // b
    return a, b


def tile_compute(rt, wt, order, place, points, h, w, frames_all, cycle):
    ordered_weight = jnp.take(wt, order, axis=0)
    background = jnp.zeros((rt.shape[0], h, w), jnp.float32)
    for index, (dy, dx) in enumerate(points):
        window = rt[:, HALO + dy : HALO + dy + h, HALO + dx : HALO + dx + w]
        background = background + ordered_weight[index][None] * window
    error = rt[:, HALO : HALO + h, HALO : HALO + w] - background
    grads = jnp.stack(
        [
            jnp.sum(error * rt[:, HALO + dy : HALO + dy + h, HALO + dx : HALO + dx + w], axis=0)
            for dy, dx in points
        ]
    )
    squares = jnp.sum(rt * rt, axis=0)
    energy_sum = jnp.zeros((h, w), jnp.float32)
    for dy, dx in points:
        energy_sum = energy_sum + squares[HALO + dy : HALO + dy + h, HALO + dx : HALO + dx + w]
    gradient = jnp.take(grads, place, axis=0)
    energy = energy_sum / (cycle * frames_all) + 1e-06
    new_weight = wt + gradient / (frames_all * energy)[None]
    return error, new_weight


def on_device(residual, cycle_weight, cycle_offsets):
    frames_dev, rows_dev, cols = residual.shape
    k_dev = cycle_weight.shape[0]
    cycle = cycle_offsets.shape[0]
    n = lax.axis_size("tm")
    frames_all = frames_dev * n
    points = cycle_points()
    same = matching(cycle_offsets, points)
    ks = jnp.arange(cycle, dtype=jnp.int32)
    order = jnp.sum(same * ks[None, :], axis=1)
    place = jnp.sum(same * ks[:, None], axis=0)

    a, b = tile_split(n, rows_dev, cols)
    h, w = rows_dev // a, cols // b

    extended = with_halo(residual, (("rows", 1),), HALO)
    padded = jnp.pad(extended, ((0, 0), (0, 0), (HALO, HALO)))
    hh, ww = h + 2 * HALO, w + 2 * HALO
    res_tiles = jnp.stack(
        [
            padded[:, i * h : i * h + hh, j * w : j * w + ww]
            for i in range(a)
            for j in range(b)
        ]
    )
    w_tiles = cycle_weight.reshape(k_dev, a, h, b, w).transpose(1, 3, 0, 2, 4)
    res_len = frames_dev * hh * ww
    w_len = k_dev * h * w
    chunk = -(-(res_len + w_len) // 1024) * 1024
    send = jnp.concatenate(
        [
            res_tiles.reshape(n, res_len),
            w_tiles.reshape(n, w_len),
            jnp.zeros((n, chunk - res_len - w_len), jnp.float32),
        ],
        axis=1,
    ).reshape(n, chunk // 128, 128)
    got = lax.all_to_all(send, "tm", 0, 0, tiled=True).reshape(n, chunk)
    rt = got[:, :res_len].reshape(frames_all, hh, ww)
    wt = got[:, res_len : res_len + w_len].reshape(cycle, h, w)

    error_t, new_t = tile_compute(rt, wt, order, place, points, h, w, frames_all, cycle)

    out = jnp.concatenate(
        [new_t.reshape(n, k_dev, h, w), error_t.reshape(n, frames_dev, h, w)], axis=1
    )
    out = lax.all_to_all(out, "tm", 0, 0, tiled=True)
    out = out.reshape(a, b, k_dev + frames_dev, h, w).transpose(2, 0, 3, 1, 4)
    out = out.reshape(k_dev + frames_dev, rows_dev, cols)
    return out[:k_dev], out[k_dev:]


def solution(mesh):
    in_specs = (P("tm", "rows", None), P("tm", "rows", None), P())
    out_specs = (P("tm", "rows", None), P("tm", "rows", None))
    return jax.shard_map(
        on_device, mesh=mesh, in_specs=in_specs, out_specs=out_specs, check_vma=False
    )
```

```python
import jax
import jax.numpy as jnp
import numpy as np
from jax import lax
from jax.sharding import PartitionSpec as P


HALO = 6


def with_halo(cells, sides, width):
    for axis, dim in sides:
        count = lax.axis_size(axis)
        ends = count - 1
        head = lax.slice_in_dim(cells, 0, width, axis=dim)
        tail = lax.slice_in_dim(cells, cells.shape[dim] - width, cells.shape[dim], axis=dim)
        cells = jnp.concatenate(
            [
                lax.ppermute(tail, axis, [(i, (i + 1) % count) for i in range(ends)]),
                cells,
                lax.ppermute(head, axis, [((i + 1) % count, i) for i in range(ends)]),
            ],
            axis=dim,
        )
    return cells


def cycle_points():
    points = []
    for row_off in range(-6, 7):
        for col_off in range(-6, 7):
            radius = row_off * row_off + col_off * col_off
            if radius >= 17 and radius <= 36:
                points.append((row_off, col_off))
    return points


def matching(cycle_offsets, points):
    table_rows = jnp.asarray(np.array([p[0] for p in points], dtype=np.int32))
    table_cols = jnp.asarray(np.array([p[1] for p in points], dtype=np.int32))
    same = (table_rows[:, None] == cycle_offsets[None, :, 0]) & (
        table_cols[:, None] == cycle_offsets[None, :, 1]
    )
    return same.astype(jnp.int32)


def tile_split(count, cols):
    b = 1
    while b * 2 <= count and cols // (b * 2) >= 128 and count % (b * 2) == 0:
        b *= 2
    a = count // b
    return a, b


def tile_partial(rt, ordered_weight, points, h, w):
    background = jnp.zeros((rt.shape[0], h, w), jnp.float32)
    for index, (dy, dx) in enumerate(points):
        window = rt[:, HALO + dy : HALO + dy + h, HALO + dx : HALO + dx + w]
        background = background + ordered_weight[index][None] * window
    error = rt[:, HALO : HALO + h, HALO : HALO + w] - background
    grads = jnp.stack(
        [
            jnp.sum(error * rt[:, HALO + dy : HALO + dy + h, HALO + dx : HALO + dx + w], axis=0)
            for dy, dx in points
        ]
    )
    squares = jnp.sum(rt * rt, axis=0)
    return error, grads, squares


def pack(parts, n):
    flat = [p.reshape(n, -1) for p in parts]
    used = sum(f.shape[1] for f in flat)
    chunk = -(-used // 1024) * 1024
    flat.append(jnp.zeros((n, chunk - used), jnp.float32))
    return jnp.concatenate(flat, axis=1).reshape(n, chunk // 128, 128)


def on_device_body(residual, cycle_weight, cycle_offsets):
    frames_dev, rows_dev, cols = residual.shape
    k_dev = cycle_weight.shape[0]
    cycle = cycle_offsets.shape[0]
    n = lax.axis_size("tm")
    frames_all = frames_dev * n
    points = cycle_points()
    same = matching(cycle_offsets, points)
    ks = jnp.arange(cycle, dtype=jnp.int32)
    order = jnp.sum(same * ks[None, :], axis=1)
    place = jnp.sum(same * ks[:, None], axis=0)

    a, b = tile_split(n, cols)
    h, w = rows_dev // a, cols // b

    extended = with_halo(residual, (("rows", 1),), HALO)
    padded = jnp.pad(extended, ((0, 0), (0, 0), (HALO, HALO)))
    hh, ww = h + 2 * HALO, w + 2 * HALO
    res_tiles = jnp.stack(
        [
            padded[:, i * h : i * h + hh, j * w : j * w + ww]
            for i in range(a)
            for j in range(b)
        ]
    )
    w_tiles = cycle_weight.reshape(k_dev, a, h, b, w).transpose(1, 3, 0, 2, 4)
    half = frames_dev // 2
    res_len = half * hh * ww
    w_len = k_dev * h * w

    got_a = lax.all_to_all(pack([w_tiles, res_tiles[:, :half]], n), "tm", 0, 0, tiled=True)
    got_a = got_a.reshape(n, -1)
    wt = got_a[:, :w_len].reshape(cycle, h, w)
    rt_a = got_a[:, w_len : w_len + res_len].reshape(n * half, hh, ww)
    got_b = lax.all_to_all(pack([res_tiles[:, half:]], n), "tm", 0, 0, tiled=True)
    rt_b = got_b.reshape(n, -1)[:, :res_len].reshape(n * half, hh, ww)

    ordered_weight = jnp.take(wt, order, axis=0)
    error_a, grads_a, squares_a = tile_partial(rt_a, ordered_weight, points, h, w)
    back_a = lax.all_to_all(error_a.reshape(n, half, h, w), "tm", 0, 0, tiled=True)
    error_b, grads_b, squares_b = tile_partial(rt_b, ordered_weight, points, h, w)

    squares = squares_a + squares_b
    energy_sum = jnp.zeros((h, w), jnp.float32)
    for dy, dx in points:
        energy_sum = energy_sum + squares[HALO + dy : HALO + dy + h, HALO + dx : HALO + dx + w]
    gradient = jnp.take(grads_a + grads_b, place, axis=0)
    energy = energy_sum / (cycle * frames_all) + 1e-06
    new_t = wt + gradient / (frames_all * energy)[None]

    out = jnp.concatenate(
        [new_t.reshape(n, k_dev, h, w), error_b.reshape(n, frames_dev - half, h, w)], axis=1
    )
    back_b = lax.all_to_all(out, "tm", 0, 0, tiled=True)

    def untile(x, lead):
        x = x.reshape(a, b, lead, h, w).transpose(2, 0, 3, 1, 4)
        return x.reshape(lead, rows_dev, cols)

    new_weight = untile(back_b[:, :k_dev], k_dev)
    error = jnp.concatenate(
        [untile(back_a, half), untile(back_b[:, k_dev:], frames_dev - half)], axis=0
    )
    return new_weight, error


def solution(mesh):
    in_specs = (P("tm", "rows", None), P("tm", "rows", None), P())
    out_specs = (P("tm", "rows", None), P("tm", "rows", None))
    return jax.shard_map(
        on_device_body, mesh=mesh, in_specs=in_specs, out_specs=out_specs, check_vma=False
    )
```

```python
import functools

import jax
import jax.numpy as jnp
import numpy as np
from jax import lax
from jax.experimental import pallas as pl
from jax.experimental.pallas import tpu as pltpu
from jax.sharding import PartitionSpec as P

HALO = 6


def with_halo(cells, sides, width):
    for axis, dim in sides:
        count = lax.axis_size(axis)
        ends = count - 1
        head = lax.slice_in_dim(cells, 0, width, axis=dim)
        tail = lax.slice_in_dim(cells, cells.shape[dim] - width, cells.shape[dim], axis=dim)
        cells = jnp.concatenate(
            [
                lax.ppermute(tail, axis, [(i, (i + 1) % count) for i in range(ends)]),
                cells,
                lax.ppermute(head, axis, [((i + 1) % count, i) for i in range(ends)]),
            ],
            axis=dim,
        )
    return cells


def cycle_points():
    points = []
    for row_off in range(-6, 7):
        for col_off in range(-6, 7):
            radius = row_off * row_off + col_off * col_off
            if radius >= 17 and radius <= 36:
                points.append((row_off, col_off))
    return points


def matching(cycle_offsets, points):
    table_rows = jnp.asarray(np.array([p[0] for p in points], dtype=np.int32))
    table_cols = jnp.asarray(np.array([p[1] for p in points], dtype=np.int32))
    same = (table_rows[:, None] == cycle_offsets[None, :, 0]) & (
        table_cols[:, None] == cycle_offsets[None, :, 1]
    )
    return same.astype(jnp.int32)


def tile_split(count, rows, cols):
    b = 1
    while b * 2 <= count and cols // (b * 2) >= 128 and count % (b * 2) == 0:
        b *= 2
    a = count // b
    return a, b


GROUP = 8


def tile_kernel(points, h, w, rt_ref, w_ref, err_ref, grad_ref):
    frames = rt_ref.shape[0]
    grad_ref[...] = jnp.zeros(grad_ref.shape, jnp.float32)

    def group(gi, carry):
        f0 = pl.multiple_of(gi * GROUP, GROUP)
        frames_here = pl.ds(f0, GROUP)
        background = jnp.zeros((GROUP, h, w), jnp.float32)
        for index, (dy, dx) in enumerate(points):
            window = rt_ref[frames_here, pl.ds(HALO + dy, h), pl.ds(HALO + dx, w)]
            background = background + w_ref[index][None] * window
        error = rt_ref[frames_here, pl.ds(HALO, h), pl.ds(HALO, w)] - background
        err_ref[frames_here] = error
        for index, (dy, dx) in enumerate(points):
            window = rt_ref[frames_here, pl.ds(HALO + dy, h), pl.ds(HALO + dx, w)]
            grad_ref[index] = grad_ref[index] + jnp.sum(error * window, axis=0)
        return carry

    lax.fori_loop(0, frames // GROUP, group, 0)


def tile_terms(rt, ordered_weight, points, h, w):
    frames = rt.shape[0]
    cycle = ordered_weight.shape[0]
    vmem = pl.BlockSpec(memory_space=pltpu.VMEM)
    return pl.pallas_call(
        functools.partial(tile_kernel, points, h, w),
        out_shape=(
            jax.ShapeDtypeStruct((frames, h, w), jnp.float32),
            jax.ShapeDtypeStruct((cycle, h, w), jnp.float32),
        ),
        in_specs=[vmem, vmem],
        out_specs=(vmem, vmem),
        cost_estimate=pl.CostEstimate(
            flops=4 * frames * cycle * h * w,
            bytes_accessed=4 * (rt.size + ordered_weight.size + (frames + cycle) * h * w),
            transcendentals=0,
        ),
    )(rt, ordered_weight)


def tile_compute(rt, wt, order, place, points, h, w, frames_all, cycle):
    ordered_weight = jnp.take(wt, order, axis=0)
    error, grads = tile_terms(rt, ordered_weight, points, h, w)
    squares = jnp.sum(rt * rt, axis=0)
    energy_sum = jnp.zeros((h, w), jnp.float32)
    for dy, dx in points:
        energy_sum = energy_sum + squares[HALO + dy : HALO + dy + h, HALO + dx : HALO + dx + w]
    gradient = jnp.take(grads, place, axis=0)
    energy = energy_sum / (cycle * frames_all) + 1e-06
    new_weight = wt + gradient / (frames_all * energy)[None]
    return error, new_weight


def on_device(residual, cycle_weight, cycle_offsets):
    frames_dev, rows_dev, cols = residual.shape
    k_dev = cycle_weight.shape[0]
    cycle = cycle_offsets.shape[0]
    n = lax.axis_size("tm")
    frames_all = frames_dev * n
    points = cycle_points()
    same = matching(cycle_offsets, points)
    ks = jnp.arange(cycle, dtype=jnp.int32)
    order = jnp.sum(same * ks[None, :], axis=1)
    place = jnp.sum(same * ks[:, None], axis=0)

    a, b = tile_split(n, rows_dev, cols)
    h, w = rows_dev // a, cols // b

    extended = with_halo(residual, (("rows", 1),), HALO)
    padded = jnp.pad(extended, ((0, 0), (0, 0), (HALO, HALO)))
    hh, ww = h + 2 * HALO, w + 2 * HALO
    res_tiles = jnp.stack(
        [
            padded[:, i * h : i * h + hh, j * w : j * w + ww]
            for i in range(a)
            for j in range(b)
        ]
    )
    w_tiles = cycle_weight.reshape(k_dev, a, h, b, w).transpose(1, 3, 0, 2, 4)
    res_len = frames_dev * hh * ww
    w_len = k_dev * h * w
    chunk = -(-(res_len + w_len) // 1024) * 1024
    send = jnp.concatenate(
        [
            res_tiles.reshape(n, res_len),
            w_tiles.reshape(n, w_len),
            jnp.zeros((n, chunk - res_len - w_len), jnp.float32),
        ],
        axis=1,
    ).reshape(n, chunk // 128, 128)
    got = lax.all_to_all(send, "tm", 0, 0, tiled=True).reshape(n, chunk)
    rt = got[:, :res_len].reshape(frames_all, hh, ww)
    wt = got[:, res_len : res_len + w_len].reshape(cycle, h, w)

    error_t, new_t = tile_compute(rt, wt, order, place, points, h, w, frames_all, cycle)

    out = jnp.concatenate(
        [new_t.reshape(n, k_dev, h, w), error_t.reshape(n, frames_dev, h, w)], axis=1
    )
    out = lax.all_to_all(out, "tm", 0, 0, tiled=True)
    out = out.reshape(a, b, k_dev + frames_dev, h, w).transpose(2, 0, 3, 1, 4)
    out = out.reshape(k_dev + frames_dev, rows_dev, cols)
    return out[:k_dev], out[k_dev:]


def solution(mesh):
    in_specs = (P("tm", "rows", None), P("tm", "rows", None), P())
    out_specs = (P("tm", "rows", None), P("tm", "rows", None))
    return jax.shard_map(
        on_device, mesh=mesh, in_specs=in_specs, out_specs=out_specs, check_vma=False
    )
```

```python
import jax
import jax.numpy as jnp
import numpy as np
from jax import lax
from jax.sharding import PartitionSpec as P

HALO = 6


def with_halo(cells, sides, width):
    for axis, dim in sides:
        count = lax.axis_size(axis)
        ends = count - 1
        head = lax.slice_in_dim(cells, 0, width, axis=dim)
        tail = lax.slice_in_dim(cells, cells.shape[dim] - width, cells.shape[dim], axis=dim)
        cells = jnp.concatenate(
            [
                lax.ppermute(tail, axis, [(i, (i + 1) % count) for i in range(ends)]),
                cells,
                lax.ppermute(head, axis, [((i + 1) % count, i) for i in range(ends)]),
            ],
            axis=dim,
        )
    return cells


def cycle_points():
    points = []
    for row_off in range(-6, 7):
        for col_off in range(-6, 7):
            radius = row_off * row_off + col_off * col_off
            if radius >= 17 and radius <= 36:
                points.append((row_off, col_off))
    return points


def matching(cycle_offsets, points):
    table_rows = jnp.asarray(np.array([p[0] for p in points], dtype=np.int32))
    table_cols = jnp.asarray(np.array([p[1] for p in points], dtype=np.int32))
    same = (table_rows[:, None] == cycle_offsets[None, :, 0]) & (
        table_cols[:, None] == cycle_offsets[None, :, 1]
    )
    return same.astype(jnp.int32)


def tile_split(count, rows, cols):
    b = 1
    while b * 2 <= count and cols // (b * 2) >= 128 and count % (b * 2) == 0:
        b *= 2
    a = count // b
    return a, b


def tile_compute(rt, wt, order, place, points, h, w, frames_all, cycle):
    ordered_weight = jnp.take(wt, order, axis=0)
    background = jnp.zeros((rt.shape[0], h, w), jnp.float32)
    for index, (dy, dx) in enumerate(points):
        window = rt[:, HALO + dy : HALO + dy + h, HALO + dx : HALO + dx + w]
        background = background + ordered_weight[index][None] * window
    error = rt[:, HALO : HALO + h, HALO : HALO + w] - background
    grads = jnp.stack(
        [
            jnp.sum(error * rt[:, HALO + dy : HALO + dy + h, HALO + dx : HALO + dx + w], axis=0)
            for dy, dx in points
        ]
    )
    squares = jnp.sum(rt * rt, axis=0)
    energy_sum = jnp.zeros((h, w), jnp.float32)
    for dy, dx in points:
        energy_sum = energy_sum + squares[HALO + dy : HALO + dy + h, HALO + dx : HALO + dx + w]
    gradient = jnp.take(grads, place, axis=0)
    energy = energy_sum / (cycle * frames_all) + 1e-06
    new_weight = wt + gradient / (frames_all * energy)[None]
    return error, new_weight


def on_device(residual, cycle_weight, cycle_offsets):
    frames_dev, rows_dev, cols = residual.shape
    k_dev = cycle_weight.shape[0]
    cycle = cycle_offsets.shape[0]
    n = lax.axis_size("tm")
    frames_all = frames_dev * n
    points = cycle_points()
    same = matching(cycle_offsets, points)
    ks = jnp.arange(cycle, dtype=jnp.int32)
    order = jnp.sum(same * ks[None, :], axis=1)
    place = jnp.sum(same * ks[:, None], axis=0)

    a, b = tile_split(n, rows_dev, cols)
    h, w = rows_dev // a, cols // b

    extended = with_halo(residual, (("rows", 1),), HALO)
    padded = jnp.pad(extended, ((0, 0), (0, 0), (HALO, HALO)))
    hh, ww = h + 2 * HALO, w + 2 * HALO
    lanes = 128
    spare = ww - lanes
    tiles = [(i, j) for i in range(a) for j in range(b)]
    main = jnp.stack([padded[:, i * h : i * h + hh, j * w : j * w + lanes] for i, j in tiles])
    rest = jnp.stack(
        [padded[:, i * h : i * h + hh, j * w + lanes : j * w + ww] for i, j in tiles]
    )
    w_tiles = cycle_weight.reshape(k_dev, a, h, b, w).transpose(1, 3, 0, 2, 4)
    main_rows = frames_dev * hh
    w_rows = k_dev * h
    rest_len = frames_dev * hh * spare
    rest_rows = -(-rest_len // lanes)
    used = main_rows + w_rows + rest_rows
    total = -(-used // 8) * 8
    send = jnp.concatenate(
        [
            main.reshape(n, main_rows, lanes),
            w_tiles.reshape(n, w_rows, lanes),
            jnp.pad(rest.reshape(n, rest_len), ((0, 0), (0, rest_rows * lanes - rest_len))).reshape(
                n, rest_rows, lanes
            ),
            jnp.zeros((n, total - used, lanes), jnp.float32),
        ],
        axis=1,
    )
    got = lax.all_to_all(send, "tm", 0, 0, tiled=True)
    rt_main = got[:, :main_rows].reshape(frames_all, hh, lanes)
    wt = got[:, main_rows : main_rows + w_rows].reshape(cycle, h, w)
    rt_rest = got[:, main_rows + w_rows : used].reshape(n, rest_rows * lanes)[:, :rest_len]
    rt = jnp.concatenate([rt_main, rt_rest.reshape(frames_all, hh, spare)], axis=2)

    error_t, new_t = tile_compute(rt, wt, order, place, points, h, w, frames_all, cycle)

    out = jnp.concatenate(
        [new_t.reshape(n, k_dev, h, w), error_t.reshape(n, frames_dev, h, w)], axis=1
    )
    out = lax.all_to_all(out, "tm", 0, 0, tiled=True)

    def untile(x, lead):
        x = x.reshape(a, b, lead, h, w).transpose(2, 0, 3, 1, 4)
        return x.reshape(lead, rows_dev, cols)

    return untile(out[:, :k_dev], k_dev), untile(out[:, k_dev:], frames_dev)


def solution(mesh):
    in_specs = (P("tm", "rows", None), P("tm", "rows", None), P())
    out_specs = (P("tm", "rows", None), P("tm", "rows", None))
    return jax.shard_map(
        on_device, mesh=mesh, in_specs=in_specs, out_specs=out_specs, check_vma=False
    )
```

```python
import functools

import jax
import jax.numpy as jnp
import numpy as np
from jax import lax
from jax.experimental import pallas as pl
from jax.experimental.pallas import tpu as pltpu
from jax.sharding import PartitionSpec as P

HALO = 6


def with_halo(cells, sides, width):
    for axis, dim in sides:
        count = lax.axis_size(axis)
        ends = count - 1
        head = lax.slice_in_dim(cells, 0, width, axis=dim)
        tail = lax.slice_in_dim(cells, cells.shape[dim] - width, cells.shape[dim], axis=dim)
        cells = jnp.concatenate(
            [
                lax.ppermute(tail, axis, [(i, (i + 1) % count) for i in range(ends)]),
                cells,
                lax.ppermute(head, axis, [((i + 1) % count, i) for i in range(ends)]),
            ],
            axis=dim,
        )
    return cells


def cycle_points():
    points = []
    for row_off in range(-6, 7):
        for col_off in range(-6, 7):
            radius = row_off * row_off + col_off * col_off
            if radius >= 17 and radius <= 36:
                points.append((row_off, col_off))
    return points


def matching(cycle_offsets, points):
    table_rows = jnp.asarray(np.array([p[0] for p in points], dtype=np.int32))
    table_cols = jnp.asarray(np.array([p[1] for p in points], dtype=np.int32))
    same = (table_rows[:, None] == cycle_offsets[None, :, 0]) & (
        table_cols[:, None] == cycle_offsets[None, :, 1]
    )
    return same.astype(jnp.int32)


def tile_split(count, rows, cols):
    b = 1
    while b * 2 <= count and cols // (b * 2) >= 128 and count % (b * 2) == 0:
        b *= 2
    a = count // b
    return a, b


def tile_compute(rt, wt, order, place, points, h, w, frames_all, cycle):
    ordered_weight = jnp.take(wt, order, axis=0)
    background = jnp.zeros((rt.shape[0], h, w), jnp.float32)
    for index, (dy, dx) in enumerate(points):
        window = rt[:, HALO + dy : HALO + dy + h, HALO + dx : HALO + dx + w]
        background = background + ordered_weight[index][None] * window
    error = rt[:, HALO : HALO + h, HALO : HALO + w] - background
    grads = jnp.stack(
        [
            jnp.sum(error * rt[:, HALO + dy : HALO + dy + h, HALO + dx : HALO + dx + w], axis=0)
            for dy, dx in points
        ]
    )
    squares = jnp.sum(rt * rt, axis=0)
    energy_sum = jnp.zeros((h, w), jnp.float32)
    for dy, dx in points:
        energy_sum = energy_sum + squares[HALO + dy : HALO + dy + h, HALO + dx : HALO + dx + w]
    gradient = jnp.take(grads, place, axis=0)
    energy = energy_sum / (cycle * frames_all) + 1e-06
    new_weight = wt + gradient / (frames_all * energy)[None]
    return error, new_weight


def exchange_kernel(n, x_ref, o_ref, send_sem, recv_sem, local_sem):
    me = lax.axis_index("tm")
    row = lax.axis_index("rows")
    mesh_id = pl.DeviceIdType.MESH
    barrier = pltpu.get_barrier_semaphore()
    for step in range(1, n):
        peer = lax.rem(me + step, n)
        pl.semaphore_signal(barrier, inc=1, device_id=(row, peer), device_id_type=mesh_id)
    pl.semaphore_wait(barrier, n - 1)
    local = pltpu.make_async_copy(x_ref.at[me], o_ref.at[me], local_sem)
    local.start()
    copies = []
    for step in range(1, n):
        peer = lax.rem(me + step, n)
        copy = pltpu.make_async_remote_copy(
            src_ref=x_ref.at[peer],
            dst_ref=o_ref.at[me],
            send_sem=send_sem.at[step],
            recv_sem=recv_sem.at[step],
            device_id=(row, peer),
            device_id_type=mesh_id,
        )
        copy.start()
        copies.append(copy)
    for copy in copies:
        copy.wait()
    local.wait()


def exchange(x, n, tag):
    anywhere = pl.BlockSpec(memory_space=pl.ANY)
    return pl.pallas_call(
        functools.partial(exchange_kernel, n),
        out_shape=jax.ShapeDtypeStruct(x.shape, x.dtype),
        in_specs=[anywhere],
        out_specs=anywhere,
        scratch_shapes=[
            pltpu.SemaphoreType.DMA((n,)),
            pltpu.SemaphoreType.DMA((n,)),
            pltpu.SemaphoreType.DMA,
        ],
        compiler_params=pltpu.CompilerParams(collective_id=tag, has_side_effects=True),
        name=f"exchange_{tag}",
    )(x)


def on_device(residual, cycle_weight, cycle_offsets):
    frames_dev, rows_dev, cols = residual.shape
    k_dev = cycle_weight.shape[0]
    cycle = cycle_offsets.shape[0]
    n = lax.axis_size("tm")
    frames_all = frames_dev * n
    points = cycle_points()
    same = matching(cycle_offsets, points)
    ks = jnp.arange(cycle, dtype=jnp.int32)
    order = jnp.sum(same * ks[None, :], axis=1)
    place = jnp.sum(same * ks[:, None], axis=0)

    a, b = tile_split(n, rows_dev, cols)
    h, w = rows_dev // a, cols // b

    extended = with_halo(residual, (("rows", 1),), HALO)
    padded = jnp.pad(extended, ((0, 0), (0, 0), (HALO, HALO)))
    hh, ww = h + 2 * HALO, w + 2 * HALO
    lanes = 128
    spare = ww - lanes
    tiles = [(i, j) for i in range(a) for j in range(b)]
    main = jnp.stack([padded[:, i * h : i * h + hh, j * w : j * w + lanes] for i, j in tiles])
    rest = jnp.stack(
        [padded[:, i * h : i * h + hh, j * w + lanes : j * w + ww] for i, j in tiles]
    )
    w_tiles = cycle_weight.reshape(k_dev, a, h, b, w).transpose(1, 3, 0, 2, 4)
    main_rows = frames_dev * hh
    w_rows = k_dev * h
    rest_len = frames_dev * hh * spare
    rest_rows = -(-rest_len // lanes)
    used = main_rows + w_rows + rest_rows
    total = -(-used // 8) * 8
    send = jnp.concatenate(
        [
            main.reshape(n, main_rows, lanes),
            w_tiles.reshape(n, w_rows, lanes),
            jnp.pad(rest.reshape(n, rest_len), ((0, 0), (0, rest_rows * lanes - rest_len))).reshape(
                n, rest_rows, lanes
            ),
            jnp.zeros((n, total - used, lanes), jnp.float32),
        ],
        axis=1,
    )
    got = lax.all_to_all(send, "tm", 0, 0, tiled=True)
    rt_main = got[:, :main_rows].reshape(frames_all, hh, lanes)
    wt = got[:, main_rows : main_rows + w_rows].reshape(cycle, h, w)
    rt_rest = got[:, main_rows + w_rows : used].reshape(n, rest_rows * lanes)[:, :rest_len]
    rt = jnp.concatenate([rt_main, rt_rest.reshape(frames_all, hh, spare)], axis=2)

    error_t, new_t = tile_compute(rt, wt, order, place, points, h, w, frames_all, cycle)

    out = jnp.concatenate(
        [new_t.reshape(n, k_dev, h, w), error_t.reshape(n, frames_dev, h, w)], axis=1
    )
    out = exchange(out.reshape(n, (k_dev + frames_dev) * h, w), n, 1)
    out = out.reshape(n, k_dev + frames_dev, h, w)

    def untile(x, lead):
        x = x.reshape(a, b, lead, h, w).transpose(2, 0, 3, 1, 4)
        return x.reshape(lead, rows_dev, cols)

    return untile(out[:, :k_dev], k_dev), untile(out[:, k_dev:], frames_dev)


def solution(mesh):
    in_specs = (P("tm", "rows", None), P("tm", "rows", None), P())
    out_specs = (P("tm", "rows", None), P("tm", "rows", None))
    return jax.shard_map(
        on_device, mesh=mesh, in_specs=in_specs, out_specs=out_specs, check_vma=False
    )
```

```python
import functools

import jax
import jax.numpy as jnp
import numpy as np
from jax import lax
from jax.experimental import pallas as pl
from jax.experimental.pallas import tpu as pltpu
from jax.sharding import PartitionSpec as P

HALO = 6


def with_halo(cells, sides, width):
    for axis, dim in sides:
        count = lax.axis_size(axis)
        ends = count - 1
        head = lax.slice_in_dim(cells, 0, width, axis=dim)
        tail = lax.slice_in_dim(cells, cells.shape[dim] - width, cells.shape[dim], axis=dim)
        cells = jnp.concatenate(
            [
                lax.ppermute(tail, axis, [(i, (i + 1) % count) for i in range(ends)]),
                cells,
                lax.ppermute(head, axis, [((i + 1) % count, i) for i in range(ends)]),
            ],
            axis=dim,
        )
    return cells


def cycle_points():
    points = []
    for row_off in range(-6, 7):
        for col_off in range(-6, 7):
            radius = row_off * row_off + col_off * col_off
            if radius >= 17 and radius <= 36:
                points.append((row_off, col_off))
    return points


def matching(cycle_offsets, points):
    table_rows = jnp.asarray(np.array([p[0] for p in points], dtype=np.int32))
    table_cols = jnp.asarray(np.array([p[1] for p in points], dtype=np.int32))
    same = (table_rows[:, None] == cycle_offsets[None, :, 0]) & (
        table_cols[:, None] == cycle_offsets[None, :, 1]
    )
    return same.astype(jnp.int32)


def tile_split(count, rows, cols):
    b = 1
    while b * 2 <= count and cols // (b * 2) >= 128 and count % (b * 2) == 0:
        b *= 2
    a = count // b
    return a, b


def tile_compute(rt, wt, order, place, points, h, w, frames_all, cycle):
    ordered_weight = jnp.take(wt, order, axis=0)
    background = jnp.zeros((rt.shape[0], h, w), jnp.float32)
    for index, (dy, dx) in enumerate(points):
        window = rt[:, HALO + dy : HALO + dy + h, HALO + dx : HALO + dx + w]
        background = background + ordered_weight[index][None] * window
    error = rt[:, HALO : HALO + h, HALO : HALO + w] - background
    grads = jnp.stack(
        [
            jnp.sum(error * rt[:, HALO + dy : HALO + dy + h, HALO + dx : HALO + dx + w], axis=0)
            for dy, dx in points
        ]
    )
    squares = jnp.sum(rt * rt, axis=0)
    energy_sum = jnp.zeros((h, w), jnp.float32)
    for dy, dx in points:
        energy_sum = energy_sum + squares[HALO + dy : HALO + dy + h, HALO + dx : HALO + dx + w]
    gradient = jnp.take(grads, place, axis=0)
    energy = energy_sum / (cycle * frames_all) + 1e-06
    new_weight = wt + gradient / (frames_all * energy)[None]
    return error, new_weight


def exchange_kernel(n, x_ref, o_ref, send_sem, recv_sem, local_sem):
    me = lax.axis_index("tm")
    row = lax.axis_index("rows")
    mesh_id = pl.DeviceIdType.MESH
    barrier = pltpu.get_barrier_semaphore()
    for step in range(1, n):
        peer = lax.rem(me + step, n)
        pl.semaphore_signal(barrier, inc=1, device_id=(row, peer), device_id_type=mesh_id)
    pl.semaphore_wait(barrier, n - 1)
    local = pltpu.make_async_copy(x_ref.at[me], o_ref.at[me], local_sem)
    local.start()
    copies = []
    for step in range(1, n):
        peer = lax.rem(me + step, n)
        copy = pltpu.make_async_remote_copy(
            src_ref=x_ref.at[peer],
            dst_ref=o_ref.at[me],
            send_sem=send_sem.at[step],
            recv_sem=recv_sem.at[step],
            device_id=(row, peer),
            device_id_type=mesh_id,
        )
        copy.start()
        copies.append(copy)
    for copy in copies:
        copy.wait()
    local.wait()


def exchange(x, n, tag):
    anywhere = pl.BlockSpec(memory_space=pl.ANY)
    return pl.pallas_call(
        functools.partial(exchange_kernel, n),
        out_shape=jax.ShapeDtypeStruct(x.shape, x.dtype),
        in_specs=[anywhere],
        out_specs=anywhere,
        scratch_shapes=[
            pltpu.SemaphoreType.DMA((n,)),
            pltpu.SemaphoreType.DMA((n,)),
            pltpu.SemaphoreType.DMA,
        ],
        compiler_params=pltpu.CompilerParams(collective_id=tag, has_side_effects=True),
        name=f"exchange_{tag}",
    )(x)


def on_device(residual, cycle_weight, cycle_offsets):
    frames_dev, rows_dev, cols = residual.shape
    k_dev = cycle_weight.shape[0]
    cycle = cycle_offsets.shape[0]
    n = lax.axis_size("tm")
    frames_all = frames_dev * n
    points = cycle_points()
    same = matching(cycle_offsets, points)
    ks = jnp.arange(cycle, dtype=jnp.int32)
    order = jnp.sum(same * ks[None, :], axis=1)
    place = jnp.sum(same * ks[:, None], axis=0)

    a, b = tile_split(n, rows_dev, cols)
    h, w = rows_dev // a, cols // b

    extended = with_halo(residual, (("rows", 1),), HALO)
    padded = jnp.pad(extended, ((0, 0), (0, 0), (HALO, HALO)))
    hh, ww = h + 2 * HALO, w + 2 * HALO
    lanes = 128
    spare = ww - lanes
    tiles = [(i, j) for i in range(a) for j in range(b)]
    main = jnp.stack([padded[:, i * h : i * h + hh, j * w : j * w + lanes] for i, j in tiles])
    rest = jnp.stack(
        [padded[:, i * h : i * h + hh, j * w + lanes : j * w + ww] for i, j in tiles]
    )
    w_tiles = cycle_weight.reshape(k_dev, a, h, b, w).transpose(1, 3, 0, 2, 4)
    main_rows = frames_dev * hh
    w_rows = k_dev * h
    rest_len = frames_dev * hh * spare
    rest_rows = -(-rest_len // lanes)
    used = main_rows + w_rows + rest_rows
    total = -(-used // 8) * 8
    send = jnp.concatenate(
        [
            main.reshape(n, main_rows, lanes),
            w_tiles.reshape(n, w_rows, lanes),
            jnp.pad(rest.reshape(n, rest_len), ((0, 0), (0, rest_rows * lanes - rest_len))).reshape(
                n, rest_rows, lanes
            ),
            jnp.zeros((n, total - used, lanes), jnp.float32),
        ],
        axis=1,
    )
    got = exchange(send, n, 0)
    rt_main = got[:, :main_rows].reshape(frames_all, hh, lanes)
    wt = got[:, main_rows : main_rows + w_rows].reshape(cycle, h, w)
    rt_rest = got[:, main_rows + w_rows : used].reshape(n, rest_rows * lanes)[:, :rest_len]
    rt = jnp.concatenate([rt_main, rt_rest.reshape(frames_all, hh, spare)], axis=2)

    error_t, new_t = tile_compute(rt, wt, order, place, points, h, w, frames_all, cycle)

    out = jnp.concatenate(
        [new_t.reshape(n, k_dev, h, w), error_t.reshape(n, frames_dev, h, w)], axis=1
    )
    out = exchange(out.reshape(n, (k_dev + frames_dev) * h, w), n, 1)
    out = out.reshape(n, k_dev + frames_dev, h, w)

    def untile(x, lead):
        x = x.reshape(a, b, lead, h, w).transpose(2, 0, 3, 1, 4)
        return x.reshape(lead, rows_dev, cols)

    return untile(out[:, :k_dev], k_dev), untile(out[:, k_dev:], frames_dev)


def solution(mesh):
    in_specs = (P("tm", "rows", None), P("tm", "rows", None), P())
    out_specs = (P("tm", "rows", None), P("tm", "rows", None))
    return jax.shard_map(
        on_device, mesh=mesh, in_specs=in_specs, out_specs=out_specs, check_vma=False
    )
```

```python
import functools

import jax
import jax.numpy as jnp
import numpy as np
from jax import lax
from jax.experimental import pallas as pl
from jax.experimental.pallas import tpu as pltpu
from jax.sharding import PartitionSpec as P

HALO = 6


def with_halo(cells, sides, width):
    for axis, dim in sides:
        count = lax.axis_size(axis)
        ends = count - 1
        head = lax.slice_in_dim(cells, 0, width, axis=dim)
        tail = lax.slice_in_dim(cells, cells.shape[dim] - width, cells.shape[dim], axis=dim)
        cells = jnp.concatenate(
            [
                lax.ppermute(tail, axis, [(i, (i + 1) % count) for i in range(ends)]),
                cells,
                lax.ppermute(head, axis, [((i + 1) % count, i) for i in range(ends)]),
            ],
            axis=dim,
        )
    return cells


def cycle_points():
    points = []
    for row_off in range(-6, 7):
        for col_off in range(-6, 7):
            radius = row_off * row_off + col_off * col_off
            if radius >= 17 and radius <= 36:
                points.append((row_off, col_off))
    return points


def matching(cycle_offsets, points):
    table_rows = jnp.asarray(np.array([p[0] for p in points], dtype=np.int32))
    table_cols = jnp.asarray(np.array([p[1] for p in points], dtype=np.int32))
    same = (table_rows[:, None] == cycle_offsets[None, :, 0]) & (
        table_cols[:, None] == cycle_offsets[None, :, 1]
    )
    return same.astype(jnp.int32)


def tile_split(count, rows, cols):
    b = 1
    while b * 2 <= count and cols // (b * 2) >= 128 and count % (b * 2) == 0:
        b *= 2
    a = count // b
    return a, b


def tile_compute(rt, wt, order, place, points, h, w, frames_all, cycle):
    ordered_weight = jnp.take(wt, order, axis=0)
    background = jnp.zeros((rt.shape[0], h, w), jnp.float32)
    for index, (dy, dx) in enumerate(points):
        window = rt[:, HALO + dy : HALO + dy + h, HALO + dx : HALO + dx + w]
        background = background + ordered_weight[index][None] * window
    error = rt[:, HALO : HALO + h, HALO : HALO + w] - background
    grads = jnp.stack(
        [
            jnp.sum(error * rt[:, HALO + dy : HALO + dy + h, HALO + dx : HALO + dx + w], axis=0)
            for dy, dx in points
        ]
    )
    squares = jnp.sum(rt * rt, axis=0)
    energy_sum = jnp.zeros((h, w), jnp.float32)
    for dy, dx in points:
        energy_sum = energy_sum + squares[HALO + dy : HALO + dy + h, HALO + dx : HALO + dx + w]
    gradient = jnp.take(grads, place, axis=0)
    energy = energy_sum / (cycle * frames_all) + 1e-06
    new_weight = wt + gradient / (frames_all * energy)[None]
    return error, new_weight


def exchange_kernel(
    n, nz, x_ref, o_ref, relay, send_sem, recv_sem, hop_send, hop_recv, on_send, on_recv, local_sem
):
    nx = n // nz
    me = lax.axis_index("tm")
    row = lax.axis_index("rows")
    xi, zi = me // nz, me % nz
    mesh_id = pl.DeviceIdType.MESH
    rows = x_ref.shape[1]
    half = rows // 2
    far = nz // 2 if nz % 2 == 0 and nz > 2 else -1

    def peer(dx, dz):
        return lax.rem(xi + dx, nx) * nz + lax.rem(zi + dz, nz)

    barrier = pltpu.get_barrier_semaphore()
    for step in range(1, n):
        pl.semaphore_signal(
            barrier, inc=1, device_id=(row, lax.rem(me + step, n)), device_id_type=mesh_id
        )
    pl.semaphore_wait(barrier, n - 1)

    local = pltpu.make_async_copy(x_ref.at[me], o_ref.at[me], local_sem)
    local.start()
    direct = []
    for dx in range(nx):
        for dz in range(nz):
            if (dx, dz) == (0, 0) or dz == far:
                continue
            slot = dx * nz + dz
            copy = pltpu.make_async_remote_copy(
                src_ref=x_ref.at[peer(dx, dz)],
                dst_ref=o_ref.at[me],
                send_sem=send_sem.at[slot],
                recv_sem=recv_sem.at[slot],
                device_id=(row, peer(dx, dz)),
                device_id_type=mesh_id,
            )
            copy.start()
            direct.append(copy)
    hops = []
    if far > 0:
        for side, dz in enumerate((1, nz - 1)):
            for dx in range(nx):
                slot = side * nx + dx
                copy = pltpu.make_async_remote_copy(
                    src_ref=x_ref.at[peer(dx, far), pl.ds(side * half, half)],
                    dst_ref=relay.at[side, dx],
                    send_sem=hop_send.at[slot],
                    recv_sem=hop_recv.at[slot],
                    device_id=(row, peer(dx, dz)),
                    device_id_type=mesh_id,
                )
                copy.start()
                hops.append((side, dz, dx, slot, copy))
    onward = []
    for side, dz, dx, slot, copy in hops:
        copy.wait_recv()
        source = peer(-dx + nx, -dz + nz)
        nxt = pltpu.make_async_remote_copy(
            src_ref=relay.at[side, dx],
            dst_ref=o_ref.at[source, pl.ds(side * half, half)],
            send_sem=on_send.at[slot],
            recv_sem=on_recv.at[slot],
            device_id=(row, peer(0, dz)),
            device_id_type=mesh_id,
        )
        nxt.start()
        onward.append(nxt)
    for copy in direct:
        copy.wait()
    for side, dz, dx, slot, copy in hops:
        copy.wait_send()
    for copy in onward:
        copy.wait()
    local.wait()


def exchange(x, n, tag):
    nz = 4 if n % 4 == 0 else 1
    nx = n // nz
    anywhere = pl.BlockSpec(memory_space=pl.ANY)
    return pl.pallas_call(
        functools.partial(exchange_kernel, n, nz),
        out_shape=jax.ShapeDtypeStruct(x.shape, x.dtype),
        in_specs=[anywhere],
        out_specs=anywhere,
        scratch_shapes=[
            pltpu.VMEM((2, nx, x.shape[1] // 2, x.shape[2]), x.dtype),
            pltpu.SemaphoreType.DMA((n,)),
            pltpu.SemaphoreType.DMA((n,)),
            pltpu.SemaphoreType.DMA((2 * nx,)),
            pltpu.SemaphoreType.DMA((2 * nx,)),
            pltpu.SemaphoreType.DMA((2 * nx,)),
            pltpu.SemaphoreType.DMA((2 * nx,)),
            pltpu.SemaphoreType.DMA,
        ],
        compiler_params=pltpu.CompilerParams(collective_id=tag, has_side_effects=True),
        name=f"exchange_{tag}",
    )(x)


def on_device(residual, cycle_weight, cycle_offsets):
    frames_dev, rows_dev, cols = residual.shape
    k_dev = cycle_weight.shape[0]
    cycle = cycle_offsets.shape[0]
    n = lax.axis_size("tm")
    frames_all = frames_dev * n
    points = cycle_points()
    same = matching(cycle_offsets, points)
    ks = jnp.arange(cycle, dtype=jnp.int32)
    order = jnp.sum(same * ks[None, :], axis=1)
    place = jnp.sum(same * ks[:, None], axis=0)

    a, b = tile_split(n, rows_dev, cols)
    h, w = rows_dev // a, cols // b

    extended = with_halo(residual, (("rows", 1),), HALO)
    padded = jnp.pad(extended, ((0, 0), (0, 0), (HALO, HALO)))
    hh, ww = h + 2 * HALO, w + 2 * HALO
    lanes = 128
    spare = ww - lanes
    tiles = [(i, j) for i in range(a) for j in range(b)]
    main = jnp.stack([padded[:, i * h : i * h + hh, j * w : j * w + lanes] for i, j in tiles])
    rest = jnp.stack(
        [padded[:, i * h : i * h + hh, j * w + lanes : j * w + ww] for i, j in tiles]
    )
    w_tiles = cycle_weight.reshape(k_dev, a, h, b, w).transpose(1, 3, 0, 2, 4)
    main_rows = frames_dev * hh
    w_rows = k_dev * h
    rest_len = frames_dev * hh * spare
    rest_rows = -(-rest_len // lanes)
    used = main_rows + w_rows + rest_rows
    total = -(-used // 8) * 8
    send = jnp.concatenate(
        [
            main.reshape(n, main_rows, lanes),
            w_tiles.reshape(n, w_rows, lanes),
            jnp.pad(rest.reshape(n, rest_len), ((0, 0), (0, rest_rows * lanes - rest_len))).reshape(
                n, rest_rows, lanes
            ),
            jnp.zeros((n, total - used, lanes), jnp.float32),
        ],
        axis=1,
    )
    got = exchange(send, n, 0)
    rt_main = got[:, :main_rows].reshape(frames_all, hh, lanes)
    wt = got[:, main_rows : main_rows + w_rows].reshape(cycle, h, w)
    rt_rest = got[:, main_rows + w_rows : used].reshape(n, rest_rows * lanes)[:, :rest_len]
    rt = jnp.concatenate([rt_main, rt_rest.reshape(frames_all, hh, spare)], axis=2)

    error_t, new_t = tile_compute(rt, wt, order, place, points, h, w, frames_all, cycle)

    out = jnp.concatenate(
        [new_t.reshape(n, k_dev, h, w), error_t.reshape(n, frames_dev, h, w)], axis=1
    )
    out = exchange(out.reshape(n, (k_dev + frames_dev) * h, w), n, 1)
    out = out.reshape(n, k_dev + frames_dev, h, w)

    def untile(x, lead):
        x = x.reshape(a, b, lead, h, w).transpose(2, 0, 3, 1, 4)
        return x.reshape(lead, rows_dev, cols)

    return untile(out[:, :k_dev], k_dev), untile(out[:, k_dev:], frames_dev)


def solution(mesh):
    in_specs = (P("tm", "rows", None), P("tm", "rows", None), P())
    out_specs = (P("tm", "rows", None), P("tm", "rows", None))
    return jax.shard_map(
        on_device, mesh=mesh, in_specs=in_specs, out_specs=out_specs, check_vma=False
    )
```

```python
import functools

import jax
import jax.numpy as jnp
import numpy as np
from jax import lax
from jax.experimental import pallas as pl
from jax.experimental.pallas import tpu as pltpu
from jax.sharding import PartitionSpec as P

HALO = 6


def with_halo(cells, sides, width):
    for axis, dim in sides:
        count = lax.axis_size(axis)
        ends = count - 1
        head = lax.slice_in_dim(cells, 0, width, axis=dim)
        tail = lax.slice_in_dim(cells, cells.shape[dim] - width, cells.shape[dim], axis=dim)
        cells = jnp.concatenate(
            [
                lax.ppermute(tail, axis, [(i, (i + 1) % count) for i in range(ends)]),
                cells,
                lax.ppermute(head, axis, [((i + 1) % count, i) for i in range(ends)]),
            ],
            axis=dim,
        )
    return cells


def cycle_points():
    points = []
    for row_off in range(-6, 7):
        for col_off in range(-6, 7):
            radius = row_off * row_off + col_off * col_off
            if radius >= 17 and radius <= 36:
                points.append((row_off, col_off))
    return points


def matching(cycle_offsets, points):
    table_rows = jnp.asarray(np.array([p[0] for p in points], dtype=np.int32))
    table_cols = jnp.asarray(np.array([p[1] for p in points], dtype=np.int32))
    same = (table_rows[:, None] == cycle_offsets[None, :, 0]) & (
        table_cols[:, None] == cycle_offsets[None, :, 1]
    )
    return same.astype(jnp.int32)


def tile_split(count, rows, cols):
    b = 1
    while b * 2 <= count and cols // (b * 2) >= 128 and count % (b * 2) == 0:
        b *= 2
    a = count // b
    return a, b


def tile_compute(rt, wt, order, place, points, h, w, frames_all, cycle):
    ordered_weight = jnp.take(wt, order, axis=0)
    background = jnp.zeros((rt.shape[0], h, w), jnp.float32)
    for index, (dy, dx) in enumerate(points):
        window = rt[:, HALO + dy : HALO + dy + h, HALO + dx : HALO + dx + w]
        background = background + ordered_weight[index][None] * window
    error = rt[:, HALO : HALO + h, HALO : HALO + w] - background
    grads = jnp.stack(
        [
            jnp.sum(error * rt[:, HALO + dy : HALO + dy + h, HALO + dx : HALO + dx + w], axis=0)
            for dy, dx in points
        ]
    )
    squares = jnp.sum(rt * rt, axis=0)
    energy_sum = jnp.zeros((h, w), jnp.float32)
    for dy, dx in points:
        energy_sum = energy_sum + squares[HALO + dy : HALO + dy + h, HALO + dx : HALO + dx + w]
    gradient = jnp.take(grads, place, axis=0)
    energy = energy_sum / (cycle * frames_all) + 1e-06
    new_weight = wt + gradient / (frames_all * energy)[None]
    return error, new_weight


def exchange_kernel(n, x_ref, o_ref, send_sem, recv_sem, local_sem):
    me = lax.axis_index("tm")
    row = lax.axis_index("rows")
    mesh_id = pl.DeviceIdType.MESH
    barrier = pltpu.get_barrier_semaphore()
    for step in range(1, n):
        peer = lax.rem(me + step, n)
        pl.semaphore_signal(barrier, inc=1, device_id=(row, peer), device_id_type=mesh_id)
    pl.semaphore_wait(barrier, n - 1)
    local = pltpu.make_async_copy(x_ref.at[me], o_ref.at[me], local_sem)
    local.start()
    copies = []
    for step in range(1, n):
        peer = lax.rem(me + step, n)
        copy = pltpu.make_async_remote_copy(
            src_ref=x_ref.at[peer],
            dst_ref=o_ref.at[me],
            send_sem=send_sem.at[step],
            recv_sem=recv_sem.at[step],
            device_id=(row, peer),
            device_id_type=mesh_id,
        )
        copy.start()
        copies.append(copy)
    for copy in copies:
        copy.wait()
    local.wait()


def exchange(x, n, tag):
    anywhere = pl.BlockSpec(memory_space=pl.ANY)
    return pl.pallas_call(
        functools.partial(exchange_kernel, n),
        out_shape=jax.ShapeDtypeStruct(x.shape, x.dtype),
        in_specs=[anywhere],
        out_specs=anywhere,
        scratch_shapes=[
            pltpu.SemaphoreType.DMA((n,)),
            pltpu.SemaphoreType.DMA((n,)),
            pltpu.SemaphoreType.DMA,
        ],
        compiler_params=pltpu.CompilerParams(collective_id=tag, has_side_effects=True),
        name=f"exchange_{tag}",
    )(x)


def on_device(residual, cycle_weight, cycle_offsets):
    frames_dev, rows_dev, cols = residual.shape
    k_dev = cycle_weight.shape[0]
    cycle = cycle_offsets.shape[0]
    n = lax.axis_size("tm")
    frames_all = frames_dev * n
    points = cycle_points()
    same = matching(cycle_offsets, points)
    ks = jnp.arange(cycle, dtype=jnp.int32)
    order = jnp.sum(same * ks[None, :], axis=1)
    place = jnp.sum(same * ks[:, None], axis=0)

    a, b = tile_split(n, rows_dev, cols)
    h, w = rows_dev // a, cols // b

    padded = jnp.pad(residual, ((0, 0), (0, 0), (HALO, HALO)))
    ww = w + 2 * HALO
    lanes = 128
    spare = ww - lanes
    tiles = [(i, j) for i in range(a) for j in range(b)]
    main = jnp.stack([padded[:, i * h : (i + 1) * h, j * w : j * w + lanes] for i, j in tiles])
    rest = jnp.stack(
        [padded[:, i * h : (i + 1) * h, j * w + lanes : j * w + ww] for i, j in tiles]
    )
    w_tiles = cycle_weight.reshape(k_dev, a, h, b, w).transpose(1, 3, 0, 2, 4)
    main_rows = frames_dev * h
    w_rows = k_dev * h
    rest_len = frames_dev * h * spare
    rest_rows = -(-rest_len // lanes)
    used = main_rows + w_rows + rest_rows
    total = -(-used // 8) * 8
    send = jnp.concatenate(
        [
            main.reshape(n, main_rows, lanes),
            w_tiles.reshape(n, w_rows, lanes),
            jnp.pad(rest.reshape(n, rest_len), ((0, 0), (0, rest_rows * lanes - rest_len))).reshape(
                n, rest_rows, lanes
            ),
            jnp.zeros((n, total - used, lanes), jnp.float32),
        ],
        axis=1,
    )
    got = exchange(send, n, 0)
    core_main = got[:, :main_rows].reshape(frames_all, h, lanes)
    wt = got[:, main_rows : main_rows + w_rows].reshape(cycle, h, w)
    core_rest = got[:, main_rows + w_rows : used].reshape(n, rest_rows * lanes)[:, :rest_len]
    core = jnp.concatenate([core_main, core_rest.reshape(frames_all, h, spare)], axis=2)

    bands = lax.axis_size("rows")
    down, up = [], []
    for r in range(bands):
        for m in range(n):
            i, j = m // b, m % b
            if i < a - 1:
                down.append((r * n + m, r * n + m + b))
            elif r < bands - 1:
                down.append((r * n + m, (r + 1) * n + j))
            if i > 0:
                up.append((r * n + m, r * n + m - b))
            elif r > 0:
                up.append((r * n + m, (r - 1) * n + (a - 1) * b + j))
    above = lax.ppermute(core[:, h - HALO :], ("rows", "tm"), down)
    below = lax.ppermute(core[:, :HALO], ("rows", "tm"), up)
    rt = jnp.concatenate([above, core, below], axis=1)

    error_t, new_t = tile_compute(rt, wt, order, place, points, h, w, frames_all, cycle)

    out = jnp.concatenate(
        [new_t.reshape(n, k_dev, h, w), error_t.reshape(n, frames_dev, h, w)], axis=1
    )
    out = exchange(out.reshape(n, (k_dev + frames_dev) * h, w), n, 1)
    out = out.reshape(n, k_dev + frames_dev, h, w)

    def untile(x, lead):
        x = x.reshape(a, b, lead, h, w).transpose(2, 0, 3, 1, 4)
        return x.reshape(lead, rows_dev, cols)

    return untile(out[:, :k_dev], k_dev), untile(out[:, k_dev:], frames_dev)


def solution(mesh):
    in_specs = (P("tm", "rows", None), P("tm", "rows", None), P())
    out_specs = (P("tm", "rows", None), P("tm", "rows", None))
    return jax.shard_map(
        on_device, mesh=mesh, in_specs=in_specs, out_specs=out_specs, check_vma=False
    )
```

```python
import functools

import jax
import jax.numpy as jnp
import numpy as np
from jax import lax
from jax.experimental import pallas as pl
from jax.experimental.pallas import tpu as pltpu
from jax.sharding import PartitionSpec as P

HALO = 6


def with_halo(cells, sides, width):
    for axis, dim in sides:
        count = lax.axis_size(axis)
        ends = count - 1
        head = lax.slice_in_dim(cells, 0, width, axis=dim)
        tail = lax.slice_in_dim(cells, cells.shape[dim] - width, cells.shape[dim], axis=dim)
        cells = jnp.concatenate(
            [
                lax.ppermute(tail, axis, [(i, (i + 1) % count) for i in range(ends)]),
                cells,
                lax.ppermute(head, axis, [((i + 1) % count, i) for i in range(ends)]),
            ],
            axis=dim,
        )
    return cells


def cycle_points():
    points = []
    for row_off in range(-6, 7):
        for col_off in range(-6, 7):
            radius = row_off * row_off + col_off * col_off
            if radius >= 17 and radius <= 36:
                points.append((row_off, col_off))
    return points


def matching(cycle_offsets, points):
    table_rows = jnp.asarray(np.array([p[0] for p in points], dtype=np.int32))
    table_cols = jnp.asarray(np.array([p[1] for p in points], dtype=np.int32))
    same = (table_rows[:, None] == cycle_offsets[None, :, 0]) & (
        table_cols[:, None] == cycle_offsets[None, :, 1]
    )
    return same.astype(jnp.int32)


def tile_split(count, rows, cols):
    b = 1
    while b * 2 <= count and cols // (b * 2) >= 128 and count % (b * 2) == 0:
        b *= 2
    a = count // b
    return a, b


def tile_compute(rt, wt, order, place, points, h, w, frames_all, cycle):
    ordered_weight = jnp.take(wt, order, axis=0)
    background = jnp.zeros((rt.shape[0], h, w), jnp.float32)
    for index, (dy, dx) in enumerate(points):
        window = rt[:, HALO + dy : HALO + dy + h, HALO + dx : HALO + dx + w]
        background = background + ordered_weight[index][None] * window
    error = rt[:, HALO : HALO + h, HALO : HALO + w] - background
    grads = jnp.stack(
        [
            jnp.sum(error * rt[:, HALO + dy : HALO + dy + h, HALO + dx : HALO + dx + w], axis=0)
            for dy, dx in points
        ]
    )
    squares = jnp.sum(rt * rt, axis=0)
    energy_sum = jnp.zeros((h, w), jnp.float32)
    for dy, dx in points:
        energy_sum = energy_sum + squares[HALO + dy : HALO + dy + h, HALO + dx : HALO + dx + w]
    gradient = jnp.take(grads, place, axis=0)
    energy = energy_sum / (cycle * frames_all) + 1e-06
    new_weight = wt + gradient / (frames_all * energy)[None]
    return error, new_weight


def exchange_kernel(n, x_ref, o_ref, send_sem, recv_sem, local_sem):
    me = lax.axis_index("tm")
    row = lax.axis_index("rows")
    mesh_id = pl.DeviceIdType.MESH
    barrier = pltpu.get_barrier_semaphore()
    for step in range(1, n):
        peer = lax.rem(me + step, n)
        pl.semaphore_signal(barrier, inc=1, device_id=(row, peer), device_id_type=mesh_id)
    pl.semaphore_wait(barrier, n - 1)
    local = pltpu.make_async_copy(x_ref.at[me], o_ref.at[me], local_sem)
    local.start()
    copies = []
    for step in range(1, n):
        peer = lax.rem(me + step, n)
        copy = pltpu.make_async_remote_copy(
            src_ref=x_ref.at[peer],
            dst_ref=o_ref.at[me],
            send_sem=send_sem.at[step],
            recv_sem=recv_sem.at[step],
            device_id=(row, peer),
            device_id_type=mesh_id,
        )
        copy.start()
        copies.append(copy)
    for copy in copies:
        copy.wait()
    local.wait()


def exchange(x, n, tag):
    anywhere = pl.BlockSpec(memory_space=pl.ANY)
    return pl.pallas_call(
        functools.partial(exchange_kernel, n),
        out_shape=jax.ShapeDtypeStruct(x.shape, x.dtype),
        in_specs=[anywhere],
        out_specs=anywhere,
        scratch_shapes=[
            pltpu.SemaphoreType.DMA((n,)),
            pltpu.SemaphoreType.DMA((n,)),
            pltpu.SemaphoreType.DMA,
        ],
        compiler_params=pltpu.CompilerParams(collective_id=tag, has_side_effects=True),
        name=f"exchange_{tag}",
    )(x)


def on_device(residual, cycle_weight, cycle_offsets):
    frames_dev, rows_dev, cols = residual.shape
    k_dev = cycle_weight.shape[0]
    cycle = cycle_offsets.shape[0]
    n = lax.axis_size("tm")
    frames_all = frames_dev * n
    points = cycle_points()
    same = matching(cycle_offsets, points)
    ks = jnp.arange(cycle, dtype=jnp.int32)
    order = jnp.sum(same * ks[None, :], axis=1)
    place = jnp.sum(same * ks[:, None], axis=0)

    a, b = tile_split(n, rows_dev, cols)
    h, w = rows_dev // a, cols // b

    padded = jnp.pad(residual, ((0, 0), (0, 0), (HALO, HALO)))
    ww = w + 2 * HALO
    lanes = 128
    spare = ww - lanes
    tiles = [(i, j) for i in range(a) for j in range(b)]
    main = jnp.stack([padded[:, i * h : (i + 1) * h, j * w : j * w + lanes] for i, j in tiles])
    rest = jnp.stack(
        [padded[:, i * h : (i + 1) * h, j * w + lanes : j * w + ww] for i, j in tiles]
    )
    w_tiles = cycle_weight.reshape(k_dev, a, h, b, w).transpose(1, 3, 0, 2, 4)
    main_rows = frames_dev * h
    w_rows = k_dev * h
    rest_len = frames_dev * h * spare
    rest_rows = -(-rest_len // lanes)
    used = main_rows + w_rows + rest_rows
    total = -(-used // 8) * 8
    send = jnp.concatenate(
        [
            main.reshape(n, main_rows, lanes),
            w_tiles.reshape(n, w_rows, lanes),
            jnp.pad(rest.reshape(n, rest_len), ((0, 0), (0, rest_rows * lanes - rest_len))).reshape(
                n, rest_rows, lanes
            ),
            jnp.zeros((n, total - used, lanes), jnp.float32),
        ],
        axis=1,
    )
    got = exchange(send, n, 0)
    core_main = got[:, :main_rows].reshape(frames_all, h, lanes)
    wt = got[:, main_rows : main_rows + w_rows].reshape(cycle, h, w)
    core_rest = got[:, main_rows + w_rows : used].reshape(n, rest_rows * lanes)[:, :rest_len]
    core = jnp.concatenate([core_main, core_rest.reshape(frames_all, h, spare)], axis=2)

    bands = lax.axis_size("rows")
    down, up = [], []
    for r in range(bands):
        for m in range(n):
            i, j = m // b, m % b
            if i < a - 1:
                down.append((r * n + m, r * n + m + b))
            elif r < bands - 1:
                down.append((r * n + m, (r + 1) * n + j))
            if i > 0:
                up.append((r * n + m, r * n + m - b))
            elif r > 0:
                up.append((r * n + m, (r - 1) * n + (a - 1) * b + j))
    edge_len = frames_all * HALO * ww
    edge_rows = -(-edge_len // 1024) * 8

    def dense(x):
        x = jnp.pad(x.reshape(edge_len), (0, edge_rows * lanes - edge_len))
        return x.reshape(edge_rows, lanes)

    def undense(x):
        return x.reshape(edge_rows * lanes)[:edge_len].reshape(frames_all, HALO, ww)

    above = undense(lax.ppermute(dense(core[:, h - HALO :]), ("rows", "tm"), down))
    below = undense(lax.ppermute(dense(core[:, :HALO]), ("rows", "tm"), up))
    rt = jnp.concatenate([above, core, below], axis=1)

    error_t, new_t = tile_compute(rt, wt, order, place, points, h, w, frames_all, cycle)

    out = jnp.concatenate(
        [new_t.reshape(n, k_dev, h, w), error_t.reshape(n, frames_dev, h, w)], axis=1
    )
    out = exchange(out.reshape(n, (k_dev + frames_dev) * h, w), n, 1)
    out = out.reshape(n, k_dev + frames_dev, h, w)

    def untile(x, lead):
        x = x.reshape(a, b, lead, h, w).transpose(2, 0, 3, 1, 4)
        return x.reshape(lead, rows_dev, cols)

    return untile(out[:, :k_dev], k_dev), untile(out[:, k_dev:], frames_dev)


def solution(mesh):
    in_specs = (P("tm", "rows", None), P("tm", "rows", None), P())
    out_specs = (P("tm", "rows", None), P("tm", "rows", None))
    return jax.shard_map(
        on_device, mesh=mesh, in_specs=in_specs, out_specs=out_specs, check_vma=False
    )
```

```python
import functools

import jax
import jax.numpy as jnp
import numpy as np
from jax import lax
from jax.experimental import pallas as pl
from jax.experimental.pallas import tpu as pltpu
from jax.sharding import PartitionSpec as P

HALO = 6


def with_halo(cells, sides, width):
    for axis, dim in sides:
        count = lax.axis_size(axis)
        ends = count - 1
        head = lax.slice_in_dim(cells, 0, width, axis=dim)
        tail = lax.slice_in_dim(cells, cells.shape[dim] - width, cells.shape[dim], axis=dim)
        cells = jnp.concatenate(
            [
                lax.ppermute(tail, axis, [(i, (i + 1) % count) for i in range(ends)]),
                cells,
                lax.ppermute(head, axis, [((i + 1) % count, i) for i in range(ends)]),
            ],
            axis=dim,
        )
    return cells


def cycle_points():
    points = []
    for row_off in range(-6, 7):
        for col_off in range(-6, 7):
            radius = row_off * row_off + col_off * col_off
            if radius >= 17 and radius <= 36:
                points.append((row_off, col_off))
    return points


def matching(cycle_offsets, points):
    table_rows = jnp.asarray(np.array([p[0] for p in points], dtype=np.int32))
    table_cols = jnp.asarray(np.array([p[1] for p in points], dtype=np.int32))
    same = (table_rows[:, None] == cycle_offsets[None, :, 0]) & (
        table_cols[:, None] == cycle_offsets[None, :, 1]
    )
    return same.astype(jnp.int32)


def tile_split(count, rows, cols):
    b = 1
    while b * 2 <= count and cols // (b * 2) >= 128 and count % (b * 2) == 0:
        b *= 2
    a = count // b
    return a, b


def tile_compute(rt, wt, order, place, points, h, w, frames_all, cycle):
    ordered_weight = jnp.take(wt, order, axis=0)
    background = jnp.zeros((rt.shape[0], h, w), jnp.float32)
    for index, (dy, dx) in enumerate(points):
        window = rt[:, HALO + dy : HALO + dy + h, HALO + dx : HALO + dx + w]
        background = background + ordered_weight[index][None] * window
    error = rt[:, HALO : HALO + h, HALO : HALO + w] - background
    grads = jnp.stack(
        [
            jnp.sum(error * rt[:, HALO + dy : HALO + dy + h, HALO + dx : HALO + dx + w], axis=0)
            for dy, dx in points
        ]
    )
    squares = jnp.sum(rt * rt, axis=0)
    energy_sum = jnp.zeros((h, w), jnp.float32)
    for dy, dx in points:
        energy_sum = energy_sum + squares[HALO + dy : HALO + dy + h, HALO + dx : HALO + dx + w]
    gradient = jnp.take(grads, place, axis=0)
    energy = energy_sum / (cycle * frames_all) + 1e-06
    new_weight = wt + gradient / (frames_all * energy)[None]
    return error, new_weight


def exchange_kernel(n, x_ref, o_ref, send_sem, recv_sem, local_sem):
    me = lax.axis_index("tm")
    row = lax.axis_index("rows")
    mesh_id = pl.DeviceIdType.MESH
    barrier = pltpu.get_barrier_semaphore()
    for step in range(1, n):
        peer = lax.rem(me + step, n)
        pl.semaphore_signal(barrier, inc=1, device_id=(row, peer), device_id_type=mesh_id)
    pl.semaphore_wait(barrier, n - 1)
    local = pltpu.make_async_copy(x_ref.at[me], o_ref.at[me], local_sem)
    local.start()
    copies = []
    for step in range(1, n):
        peer = lax.rem(me + step, n)
        copy = pltpu.make_async_remote_copy(
            src_ref=x_ref.at[peer],
            dst_ref=o_ref.at[me],
            send_sem=send_sem.at[step],
            recv_sem=recv_sem.at[step],
            device_id=(row, peer),
            device_id_type=mesh_id,
        )
        copy.start()
        copies.append(copy)
    for copy in copies:
        copy.wait()
    local.wait()


def exchange(x, n, tag):
    anywhere = pl.BlockSpec(memory_space=pl.ANY)
    return pl.pallas_call(
        functools.partial(exchange_kernel, n),
        out_shape=jax.ShapeDtypeStruct(x.shape, x.dtype),
        in_specs=[anywhere],
        out_specs=anywhere,
        scratch_shapes=[
            pltpu.SemaphoreType.DMA((n,)),
            pltpu.SemaphoreType.DMA((n,)),
            pltpu.SemaphoreType.DMA,
        ],
        compiler_params=pltpu.CompilerParams(collective_id=tag, has_side_effects=True),
        name=f"exchange_{tag}",
    )(x)


def return_kernel(n, b, nw_ref, er_ref, nw_out, er_out, send_sem, recv_sem, local_sem):
    me = lax.axis_index("tm")
    row = lax.axis_index("rows")
    mesh_id = pl.DeviceIdType.MESH
    h, w = nw_ref.shape[2], nw_ref.shape[3]
    rows_at = pl.ds(pl.multiple_of((me // b) * h, h), h)
    cols_at = pl.ds(pl.multiple_of((me % b) * w, w), w)
    barrier = pltpu.get_barrier_semaphore()
    for step in range(1, n):
        pl.semaphore_signal(
            barrier, inc=1, device_id=(row, lax.rem(me + step, n)), device_id_type=mesh_id
        )
    pl.semaphore_wait(barrier, n - 1)
    pairs = ((nw_ref, nw_out), (er_ref, er_out))
    local = []
    for which, (src, dst) in enumerate(pairs):
        copy = pltpu.make_async_copy(src.at[me], dst.at[:, rows_at, cols_at], local_sem.at[which])
        copy.start()
        local.append(copy)
    copies = []
    for step in range(1, n):
        peer = lax.rem(me + step, n)
        for which, (src, dst) in enumerate(pairs):
            copy = pltpu.make_async_remote_copy(
                src_ref=src.at[peer],
                dst_ref=dst.at[:, rows_at, cols_at],
                send_sem=send_sem.at[which, step],
                recv_sem=recv_sem.at[which, step],
                device_id=(row, peer),
                device_id_type=mesh_id,
            )
            copy.start()
            copies.append(copy)
    for copy in copies:
        copy.wait()
    for copy in local:
        copy.wait()


def return_exchange(new_t, error_t, n, b, rows_dev, cols, tag):
    anywhere = pl.BlockSpec(memory_space=pl.ANY)
    k_dev, f_dev = new_t.shape[1], error_t.shape[1]
    return pl.pallas_call(
        functools.partial(return_kernel, n, b),
        out_shape=(
            jax.ShapeDtypeStruct((k_dev, rows_dev, cols), new_t.dtype),
            jax.ShapeDtypeStruct((f_dev, rows_dev, cols), error_t.dtype),
        ),
        in_specs=[anywhere, anywhere],
        out_specs=(anywhere, anywhere),
        scratch_shapes=[
            pltpu.SemaphoreType.DMA((2, n)),
            pltpu.SemaphoreType.DMA((2, n)),
            pltpu.SemaphoreType.DMA((2,)),
        ],
        compiler_params=pltpu.CompilerParams(collective_id=tag, has_side_effects=True),
        name=f"exchange_{tag}",
    )(new_t, error_t)


def on_device(residual, cycle_weight, cycle_offsets):
    frames_dev, rows_dev, cols = residual.shape
    k_dev = cycle_weight.shape[0]
    cycle = cycle_offsets.shape[0]
    n = lax.axis_size("tm")
    frames_all = frames_dev * n
    points = cycle_points()
    same = matching(cycle_offsets, points)
    ks = jnp.arange(cycle, dtype=jnp.int32)
    order = jnp.sum(same * ks[None, :], axis=1)
    place = jnp.sum(same * ks[:, None], axis=0)

    a, b = tile_split(n, rows_dev, cols)
    h, w = rows_dev // a, cols // b

    padded = jnp.pad(residual, ((0, 0), (0, 0), (HALO, HALO)))
    ww = w + 2 * HALO
    lanes = 128
    spare = ww - lanes
    tiles = [(i, j) for i in range(a) for j in range(b)]
    main = jnp.stack([padded[:, i * h : (i + 1) * h, j * w : j * w + lanes] for i, j in tiles])
    rest = jnp.stack(
        [padded[:, i * h : (i + 1) * h, j * w + lanes : j * w + ww] for i, j in tiles]
    )
    w_tiles = cycle_weight.reshape(k_dev, a, h, b, w).transpose(1, 3, 0, 2, 4)
    main_rows = frames_dev * h
    w_rows = k_dev * h
    rest_len = frames_dev * h * spare
    rest_rows = -(-rest_len // lanes)
    used = main_rows + w_rows + rest_rows
    total = -(-used // 8) * 8
    send = jnp.concatenate(
        [
            main.reshape(n, main_rows, lanes),
            w_tiles.reshape(n, w_rows, lanes),
            jnp.pad(rest.reshape(n, rest_len), ((0, 0), (0, rest_rows * lanes - rest_len))).reshape(
                n, rest_rows, lanes
            ),
            jnp.zeros((n, total - used, lanes), jnp.float32),
        ],
        axis=1,
    )
    got = exchange(send, n, 0)
    core_main = got[:, :main_rows].reshape(frames_all, h, lanes)
    wt = got[:, main_rows : main_rows + w_rows].reshape(cycle, h, w)
    core_rest = got[:, main_rows + w_rows : used].reshape(n, rest_rows * lanes)[:, :rest_len]
    core = jnp.concatenate([core_main, core_rest.reshape(frames_all, h, spare)], axis=2)

    bands = lax.axis_size("rows")
    down, up = [], []
    for r in range(bands):
        for m in range(n):
            i, j = m // b, m % b
            if i < a - 1:
                down.append((r * n + m, r * n + m + b))
            elif r < bands - 1:
                down.append((r * n + m, (r + 1) * n + j))
            if i > 0:
                up.append((r * n + m, r * n + m - b))
            elif r > 0:
                up.append((r * n + m, (r - 1) * n + (a - 1) * b + j))
    edge_len = frames_all * HALO * ww
    edge_rows = -(-edge_len // 1024) * 8

    def dense(x):
        x = jnp.pad(x.reshape(edge_len), (0, edge_rows * lanes - edge_len))
        return x.reshape(edge_rows, lanes)

    def undense(x):
        return x.reshape(edge_rows * lanes)[:edge_len].reshape(frames_all, HALO, ww)

    above = undense(lax.ppermute(dense(core[:, h - HALO :]), ("rows", "tm"), down))
    below = undense(lax.ppermute(dense(core[:, :HALO]), ("rows", "tm"), up))
    rt = jnp.concatenate([above, core, below], axis=1)

    error_t, new_t = tile_compute(rt, wt, order, place, points, h, w, frames_all, cycle)

    return return_exchange(
        new_t.reshape(n, k_dev, h, w), error_t.reshape(n, frames_dev, h, w), n, b, rows_dev, cols, 1
    )


def solution(mesh):
    in_specs = (P("tm", "rows", None), P("tm", "rows", None), P())
    out_specs = (P("tm", "rows", None), P("tm", "rows", None))
    return jax.shard_map(
        on_device, mesh=mesh, in_specs=in_specs, out_specs=out_specs, check_vma=False
    )
```

```python
import functools

import jax
import jax.numpy as jnp
import numpy as np
from jax import lax
from jax.experimental import pallas as pl
from jax.experimental.pallas import tpu as pltpu
from jax.sharding import PartitionSpec as P

HALO = 6


def with_halo(cells, sides, width):
    for axis, dim in sides:
        count = lax.axis_size(axis)
        ends = count - 1
        head = lax.slice_in_dim(cells, 0, width, axis=dim)
        tail = lax.slice_in_dim(cells, cells.shape[dim] - width, cells.shape[dim], axis=dim)
        cells = jnp.concatenate(
            [
                lax.ppermute(tail, axis, [(i, (i + 1) % count) for i in range(ends)]),
                cells,
                lax.ppermute(head, axis, [((i + 1) % count, i) for i in range(ends)]),
            ],
            axis=dim,
        )
    return cells


def cycle_points():
    points = []
    for row_off in range(-6, 7):
        for col_off in range(-6, 7):
            radius = row_off * row_off + col_off * col_off
            if radius >= 17 and radius <= 36:
                points.append((row_off, col_off))
    return points


def matching(cycle_offsets, points):
    table_rows = jnp.asarray(np.array([p[0] for p in points], dtype=np.int32))
    table_cols = jnp.asarray(np.array([p[1] for p in points], dtype=np.int32))
    same = (table_rows[:, None] == cycle_offsets[None, :, 0]) & (
        table_cols[:, None] == cycle_offsets[None, :, 1]
    )
    return same.astype(jnp.int32)


def tile_split(count, rows, cols):
    b = 1
    while b * 2 <= count and cols // (b * 2) >= 128 and count % (b * 2) == 0:
        b *= 2
    a = count // b
    return a, b


def tile_compute(rt, wt, order, place, points, h, w, frames_all, cycle):
    ordered_weight = jnp.take(wt, order, axis=0)
    background = jnp.zeros((rt.shape[0], h, w), jnp.float32)
    for index, (dy, dx) in enumerate(points):
        window = rt[:, HALO + dy : HALO + dy + h, HALO + dx : HALO + dx + w]
        background = background + ordered_weight[index][None] * window
    error = rt[:, HALO : HALO + h, HALO : HALO + w] - background
    grads = jnp.stack(
        [
            jnp.sum(error * rt[:, HALO + dy : HALO + dy + h, HALO + dx : HALO + dx + w], axis=0)
            for dy, dx in points
        ]
    )
    squares = jnp.sum(rt * rt, axis=0)
    energy_sum = jnp.zeros((h, w), jnp.float32)
    for dy, dx in points:
        energy_sum = energy_sum + squares[HALO + dy : HALO + dy + h, HALO + dx : HALO + dx + w]
    gradient = jnp.take(grads, place, axis=0)
    energy = energy_sum / (cycle * frames_all) + 1e-06
    new_weight = wt + gradient / (frames_all * energy)[None]
    return error, new_weight


def exchange_kernel(n, x_ref, o_ref, send_sem, recv_sem, local_sem):
    me = lax.axis_index("tm")
    row = lax.axis_index("rows")
    mesh_id = pl.DeviceIdType.MESH
    barrier = pltpu.get_barrier_semaphore()
    for step in range(1, n):
        peer = lax.rem(me + step, n)
        pl.semaphore_signal(barrier, inc=1, device_id=(row, peer), device_id_type=mesh_id)
    pl.semaphore_wait(barrier, n - 1)
    local = pltpu.make_async_copy(x_ref.at[me], o_ref.at[me], local_sem)
    local.start()
    copies = []
    for step in range(1, n):
        peer = lax.rem(me + step, n)
        copy = pltpu.make_async_remote_copy(
            src_ref=x_ref.at[peer],
            dst_ref=o_ref.at[me],
            send_sem=send_sem.at[step],
            recv_sem=recv_sem.at[step],
            device_id=(row, peer),
            device_id_type=mesh_id,
        )
        copy.start()
        copies.append(copy)
    for copy in copies:
        copy.wait()
    local.wait()


def exchange(x, n, tag):
    anywhere = pl.BlockSpec(memory_space=pl.ANY)
    return pl.pallas_call(
        functools.partial(exchange_kernel, n),
        out_shape=jax.ShapeDtypeStruct(x.shape, x.dtype),
        in_specs=[anywhere],
        out_specs=anywhere,
        scratch_shapes=[
            pltpu.SemaphoreType.DMA((n,)),
            pltpu.SemaphoreType.DMA((n,)),
            pltpu.SemaphoreType.DMA,
        ],
        compiler_params=pltpu.CompilerParams(collective_id=tag, has_side_effects=True),
        name=f"exchange_{tag}",
    )(x)


def return_kernel(n, b, nw_ref, er_ref, nw_out, er_out, send_sem, recv_sem, local_sem):
    me = lax.axis_index("tm")
    row = lax.axis_index("rows")
    mesh_id = pl.DeviceIdType.MESH
    h, w = nw_ref.shape[2], nw_ref.shape[3]
    rows_at = pl.ds(pl.multiple_of((me // b) * h, h), h)
    cols_at = pl.ds(pl.multiple_of((me % b) * w, w), w)
    barrier = pltpu.get_barrier_semaphore()
    for step in range(1, n):
        pl.semaphore_signal(
            barrier, inc=1, device_id=(row, lax.rem(me + step, n)), device_id_type=mesh_id
        )
    pl.semaphore_wait(barrier, n - 1)
    pairs = ((nw_ref, nw_out), (er_ref, er_out))
    local = []
    for which, (src, dst) in enumerate(pairs):
        copy = pltpu.make_async_copy(src.at[me], dst.at[:, rows_at, cols_at], local_sem.at[which])
        copy.start()
        local.append(copy)
    copies = []
    for step in range(1, n):
        peer = lax.rem(me + step, n)
        for which, (src, dst) in enumerate(pairs):
            copy = pltpu.make_async_remote_copy(
                src_ref=src.at[peer],
                dst_ref=dst.at[:, rows_at, cols_at],
                send_sem=send_sem.at[which, step],
                recv_sem=recv_sem.at[which, step],
                device_id=(row, peer),
                device_id_type=mesh_id,
            )
            copy.start()
            copies.append(copy)
    for copy in copies:
        copy.wait()
    for copy in local:
        copy.wait()


def return_exchange(new_t, error_t, n, b, rows_dev, cols, tag):
    anywhere = pl.BlockSpec(memory_space=pl.ANY)
    k_dev, f_dev = new_t.shape[1], error_t.shape[1]
    return pl.pallas_call(
        functools.partial(return_kernel, n, b),
        out_shape=(
            jax.ShapeDtypeStruct((k_dev, rows_dev, cols), new_t.dtype),
            jax.ShapeDtypeStruct((f_dev, rows_dev, cols), error_t.dtype),
        ),
        in_specs=[anywhere, anywhere],
        out_specs=(anywhere, anywhere),
        scratch_shapes=[
            pltpu.SemaphoreType.DMA((2, n)),
            pltpu.SemaphoreType.DMA((2, n)),
            pltpu.SemaphoreType.DMA((2,)),
        ],
        compiler_params=pltpu.CompilerParams(collective_id=tag, has_side_effects=True),
        name=f"exchange_{tag}",
    )(new_t, error_t)


def on_device(residual, cycle_weight, cycle_offsets):
    frames_dev, rows_dev, cols = residual.shape
    k_dev = cycle_weight.shape[0]
    cycle = cycle_offsets.shape[0]
    n = lax.axis_size("tm")
    frames_all = frames_dev * n
    points = cycle_points()
    same = matching(cycle_offsets, points)
    ks = jnp.arange(cycle, dtype=jnp.int32)
    order = jnp.sum(same * ks[None, :], axis=1)
    place = jnp.sum(same * ks[:, None], axis=0)

    a, b = tile_split(n, rows_dev, cols)
    h, w = rows_dev // a, cols // b

    padded = jnp.pad(residual, ((0, 0), (0, 0), (HALO, HALO)))
    ww = w + 2 * HALO
    lanes = 128
    spare = ww - lanes
    tiles = [(i, j) for i in range(a) for j in range(b)]
    main = jnp.stack([padded[:, i * h : (i + 1) * h, j * w : j * w + lanes] for i, j in tiles])
    rest = jnp.stack(
        [padded[:, i * h : (i + 1) * h, j * w + lanes : j * w + ww] for i, j in tiles]
    )
    w_tiles = cycle_weight.reshape(k_dev, a, h, b, w).transpose(1, 3, 0, 2, 4)
    main_rows = frames_dev * h
    w_rows = k_dev * h
    rest_len = frames_dev * h * spare
    rest_rows = -(-rest_len // lanes)
    used = main_rows + w_rows + rest_rows
    total = -(-used // 8) * 8
    send = jnp.concatenate(
        [
            main.reshape(n, main_rows, lanes),
            w_tiles.reshape(n, w_rows, lanes),
            jnp.pad(rest.reshape(n, rest_len), ((0, 0), (0, rest_rows * lanes - rest_len))).reshape(
                n, rest_rows, lanes
            ),
            jnp.zeros((n, total - used, lanes), jnp.float32),
        ],
        axis=1,
    )
    got = exchange(send, n, 0)
    core_main = got[:, :main_rows].reshape(frames_all, h, lanes)
    wt = got[:, main_rows : main_rows + w_rows].reshape(cycle, h, w)
    core_rest = got[:, main_rows + w_rows : used].reshape(n, rest_rows * lanes)[:, :rest_len]
    core = jnp.concatenate([core_main, core_rest.reshape(frames_all, h, spare)], axis=2)

    bands = lax.axis_size("rows")
    down, up = [], []
    for r in range(bands):
        for m in range(n):
            i, j = m // b, m % b
            if i < a - 1:
                down.append((r * n + m, r * n + m + b))
            elif r < bands - 1:
                down.append((r * n + m, (r + 1) * n + j))
            if i > 0:
                up.append((r * n + m, r * n + m - b))
            elif r > 0:
                up.append((r * n + m, (r - 1) * n + (a - 1) * b + j))
    edge_len = frames_all * HALO * ww
    edge_rows = -(-edge_len // 1024) * 8

    def dense(x):
        x = jnp.pad(x.reshape(edge_len), (0, edge_rows * lanes - edge_len))
        return x.reshape(edge_rows, lanes)

    def undense(x):
        return x.reshape(edge_rows * lanes)[:edge_len].reshape(frames_all, HALO, ww)

    above = undense(lax.ppermute(dense(core[:, h - HALO :]), ("rows", "tm"), down))
    below = undense(lax.ppermute(dense(core[:, :HALO]), ("rows", "tm"), up))
    rt = lax.optimization_barrier(jnp.concatenate([above, core, below], axis=1))

    error_t, new_t = tile_compute(rt, wt, order, place, points, h, w, frames_all, cycle)

    return return_exchange(
        new_t.reshape(n, k_dev, h, w), error_t.reshape(n, frames_dev, h, w), n, b, rows_dev, cols, 1
    )


def solution(mesh):
    in_specs = (P("tm", "rows", None), P("tm", "rows", None), P())
    out_specs = (P("tm", "rows", None), P("tm", "rows", None))
    return jax.shard_map(
        on_device, mesh=mesh, in_specs=in_specs, out_specs=out_specs, check_vma=False
    )
```

```python
import functools

import jax
import jax.numpy as jnp
import numpy as np
from jax import lax
from jax.experimental import pallas as pl
from jax.experimental.pallas import tpu as pltpu
from jax.sharding import PartitionSpec as P

HALO = 6


def with_halo(cells, sides, width):
    for axis, dim in sides:
        count = lax.axis_size(axis)
        ends = count - 1
        head = lax.slice_in_dim(cells, 0, width, axis=dim)
        tail = lax.slice_in_dim(cells, cells.shape[dim] - width, cells.shape[dim], axis=dim)
        cells = jnp.concatenate(
            [
                lax.ppermute(tail, axis, [(i, (i + 1) % count) for i in range(ends)]),
                cells,
                lax.ppermute(head, axis, [((i + 1) % count, i) for i in range(ends)]),
            ],
            axis=dim,
        )
    return cells


def cycle_points():
    points = []
    for row_off in range(-6, 7):
        for col_off in range(-6, 7):
            radius = row_off * row_off + col_off * col_off
            if radius >= 17 and radius <= 36:
                points.append((row_off, col_off))
    return points


def matching(cycle_offsets, points):
    table_rows = jnp.asarray(np.array([p[0] for p in points], dtype=np.int32))
    table_cols = jnp.asarray(np.array([p[1] for p in points], dtype=np.int32))
    same = (table_rows[:, None] == cycle_offsets[None, :, 0]) & (
        table_cols[:, None] == cycle_offsets[None, :, 1]
    )
    return same.astype(jnp.int32)


def tile_split(count, rows, cols):
    b = 1
    while b * 2 <= count and cols // (b * 2) >= 128 and count % (b * 2) == 0:
        b *= 2
    a = count // b
    return a, b


def tile_compute(rt, wt, order, place, points, h, w, frames_all, cycle):
    ordered_weight = jnp.take(wt, order, axis=0)
    background = jnp.zeros((rt.shape[0], h, w), jnp.float32)
    for index, (dy, dx) in enumerate(points):
        window = rt[:, HALO + dy : HALO + dy + h, HALO + dx : HALO + dx + w]
        background = background + ordered_weight[index][None] * window
    error = rt[:, HALO : HALO + h, HALO : HALO + w] - background
    grads = jnp.stack(
        [
            jnp.sum(error * rt[:, HALO + dy : HALO + dy + h, HALO + dx : HALO + dx + w], axis=0)
            for dy, dx in points
        ]
    )
    squares = jnp.sum(rt * rt, axis=0)
    energy_sum = jnp.zeros((h, w), jnp.float32)
    for dy, dx in points:
        energy_sum = energy_sum + squares[HALO + dy : HALO + dy + h, HALO + dx : HALO + dx + w]
    gradient = jnp.take(grads, place, axis=0)
    energy = energy_sum / (cycle * frames_all) + 1e-06
    new_weight = wt + gradient / (frames_all * energy)[None]
    return error, new_weight


def exchange_kernel(n, x_ref, o_ref, send_sem, recv_sem, local_sem):
    me = lax.axis_index("tm")
    row = lax.axis_index("rows")
    mesh_id = pl.DeviceIdType.MESH
    barrier = pltpu.get_barrier_semaphore()
    for step in range(1, n):
        peer = lax.rem(me + step, n)
        pl.semaphore_signal(barrier, inc=1, device_id=(row, peer), device_id_type=mesh_id)
    pl.semaphore_wait(barrier, n - 1)
    local = pltpu.make_async_copy(x_ref.at[me], o_ref.at[me], local_sem)
    local.start()
    copies = []
    for step in range(1, n):
        peer = lax.rem(me + step, n)
        copy = pltpu.make_async_remote_copy(
            src_ref=x_ref.at[peer],
            dst_ref=o_ref.at[me],
            send_sem=send_sem.at[step],
            recv_sem=recv_sem.at[step],
            device_id=(row, peer),
            device_id_type=mesh_id,
        )
        copy.start()
        copies.append(copy)
    for copy in copies:
        copy.wait()
    local.wait()


def exchange(x, n, tag):
    anywhere = pl.BlockSpec(memory_space=pl.ANY)
    return pl.pallas_call(
        functools.partial(exchange_kernel, n),
        out_shape=jax.ShapeDtypeStruct(x.shape, x.dtype),
        in_specs=[anywhere],
        out_specs=anywhere,
        scratch_shapes=[
            pltpu.SemaphoreType.DMA((n,)),
            pltpu.SemaphoreType.DMA((n,)),
            pltpu.SemaphoreType.DMA,
        ],
        compiler_params=pltpu.CompilerParams(collective_id=tag, has_side_effects=True),
        name=f"exchange_{tag}",
    )(x)


def return_kernel(n, b, nw_ref, er_ref, nw_out, er_out, send_sem, recv_sem, local_sem):
    me = lax.axis_index("tm")
    row = lax.axis_index("rows")
    mesh_id = pl.DeviceIdType.MESH
    h, w = nw_ref.shape[2], nw_ref.shape[3]
    rows_at = pl.ds(pl.multiple_of((me // b) * h, h), h)
    cols_at = pl.ds(pl.multiple_of((me % b) * w, w), w)
    barrier = pltpu.get_barrier_semaphore()
    for step in range(1, n):
        pl.semaphore_signal(
            barrier, inc=1, device_id=(row, lax.rem(me + step, n)), device_id_type=mesh_id
        )
    pl.semaphore_wait(barrier, n - 1)
    pairs = ((nw_ref, nw_out), (er_ref, er_out))
    local = []
    for which, (src, dst) in enumerate(pairs):
        copy = pltpu.make_async_copy(src.at[me], dst.at[:, rows_at, cols_at], local_sem.at[which])
        copy.start()
        local.append(copy)
    copies = []
    for step in range(1, n):
        peer = lax.rem(me + step, n)
        for which, (src, dst) in enumerate(pairs):
            copy = pltpu.make_async_remote_copy(
                src_ref=src.at[peer],
                dst_ref=dst.at[:, rows_at, cols_at],
                send_sem=send_sem.at[which, step],
                recv_sem=recv_sem.at[which, step],
                device_id=(row, peer),
                device_id_type=mesh_id,
            )
            copy.start()
            copies.append(copy)
    for copy in copies:
        copy.wait()
    for copy in local:
        copy.wait()


def return_exchange(new_t, error_t, n, b, rows_dev, cols, tag):
    anywhere = pl.BlockSpec(memory_space=pl.ANY)
    k_dev, f_dev = new_t.shape[1], error_t.shape[1]
    return pl.pallas_call(
        functools.partial(return_kernel, n, b),
        out_shape=(
            jax.ShapeDtypeStruct((k_dev, rows_dev, cols), new_t.dtype),
            jax.ShapeDtypeStruct((f_dev, rows_dev, cols), error_t.dtype),
        ),
        in_specs=[anywhere, anywhere],
        out_specs=(anywhere, anywhere),
        scratch_shapes=[
            pltpu.SemaphoreType.DMA((2, n)),
            pltpu.SemaphoreType.DMA((2, n)),
            pltpu.SemaphoreType.DMA((2,)),
        ],
        compiler_params=pltpu.CompilerParams(collective_id=tag, has_side_effects=True),
        name=f"exchange_{tag}",
    )(new_t, error_t)


def on_device(residual, cycle_weight, cycle_offsets):
    frames_dev, rows_dev, cols = residual.shape
    k_dev = cycle_weight.shape[0]
    cycle = cycle_offsets.shape[0]
    n = lax.axis_size("tm")
    frames_all = frames_dev * n
    points = cycle_points()
    same = matching(cycle_offsets, points)
    ks = jnp.arange(cycle, dtype=jnp.int32)
    order = jnp.sum(same * ks[None, :], axis=1)
    place = jnp.sum(same * ks[:, None], axis=0)

    a, b = tile_split(n, rows_dev, cols)
    h, w = rows_dev // a, cols // b

    padded = jnp.pad(residual, ((0, 0), (0, 0), (HALO, HALO)))
    ww = w + 2 * HALO
    lanes = 128
    spare = ww - lanes
    tiles = [(i, j) for i in range(a) for j in range(b)]
    main = jnp.stack([padded[:, i * h : (i + 1) * h, j * w : j * w + lanes] for i, j in tiles])
    rest = jnp.stack(
        [padded[:, i * h : (i + 1) * h, j * w + lanes : j * w + ww] for i, j in tiles]
    )
    w_tiles = cycle_weight.reshape(k_dev, a, h, b, w).transpose(1, 3, 0, 2, 4)
    main_rows = frames_dev * h
    w_rows = k_dev * h
    rest_len = frames_dev * h * spare
    rest_rows = -(-rest_len // lanes)
    used = main_rows + w_rows + rest_rows
    total = -(-used // 8) * 8
    send = jnp.concatenate(
        [
            main.reshape(n, main_rows, lanes),
            w_tiles.reshape(n, w_rows, lanes),
            jnp.pad(rest.reshape(n, rest_len), ((0, 0), (0, rest_rows * lanes - rest_len))).reshape(
                n, rest_rows, lanes
            ),
            jnp.zeros((n, total - used, lanes), jnp.float32),
        ],
        axis=1,
    )
    got = exchange(send, n, 0)
    core_main = got[:, :main_rows].reshape(frames_all, h, lanes)
    wt = got[:, main_rows : main_rows + w_rows].reshape(cycle, h, w)
    core_rest = got[:, main_rows + w_rows : used].reshape(n, rest_rows * lanes)[:, :rest_len]
    core = lax.optimization_barrier(
        jnp.concatenate([core_main, core_rest.reshape(frames_all, h, spare)], axis=2)
    )

    bands = lax.axis_size("rows")
    down, up = [], []
    for r in range(bands):
        for m in range(n):
            i, j = m // b, m % b
            if i < a - 1:
                down.append((r * n + m, r * n + m + b))
            elif r < bands - 1:
                down.append((r * n + m, (r + 1) * n + j))
            if i > 0:
                up.append((r * n + m, r * n + m - b))
            elif r > 0:
                up.append((r * n + m, (r - 1) * n + (a - 1) * b + j))
    edge_len = frames_all * HALO * ww
    edge_rows = -(-edge_len // 1024) * 8

    def dense(x):
        x = jnp.pad(x.reshape(edge_len), (0, edge_rows * lanes - edge_len))
        return x.reshape(edge_rows, lanes)

    def undense(x):
        return x.reshape(edge_rows * lanes)[:edge_len].reshape(frames_all, HALO, ww)

    above = undense(lax.ppermute(dense(core[:, h - HALO :]), ("rows", "tm"), down))
    below = undense(lax.ppermute(dense(core[:, :HALO]), ("rows", "tm"), up))
    rt = lax.optimization_barrier(jnp.concatenate([above, core, below], axis=1))

    error_t, new_t = tile_compute(rt, wt, order, place, points, h, w, frames_all, cycle)

    return return_exchange(
        new_t.reshape(n, k_dev, h, w), error_t.reshape(n, frames_dev, h, w), n, b, rows_dev, cols, 1
    )


def solution(mesh):
    in_specs = (P("tm", "rows", None), P("tm", "rows", None), P())
    out_specs = (P("tm", "rows", None), P("tm", "rows", None))
    return jax.shard_map(
        on_device, mesh=mesh, in_specs=in_specs, out_specs=out_specs, check_vma=False
    )
```

```python
import functools

import jax
import jax.numpy as jnp
import numpy as np
from jax import lax
from jax.experimental import pallas as pl
from jax.experimental.pallas import tpu as pltpu
from jax.sharding import PartitionSpec as P

HALO = 6


def with_halo(cells, sides, width):
    for axis, dim in sides:
        count = lax.axis_size(axis)
        ends = count - 1
        head = lax.slice_in_dim(cells, 0, width, axis=dim)
        tail = lax.slice_in_dim(cells, cells.shape[dim] - width, cells.shape[dim], axis=dim)
        cells = jnp.concatenate(
            [
                lax.ppermute(tail, axis, [(i, (i + 1) % count) for i in range(ends)]),
                cells,
                lax.ppermute(head, axis, [((i + 1) % count, i) for i in range(ends)]),
            ],
            axis=dim,
        )
    return cells


def cycle_points():
    points = []
    for row_off in range(-6, 7):
        for col_off in range(-6, 7):
            radius = row_off * row_off + col_off * col_off
            if radius >= 17 and radius <= 36:
                points.append((row_off, col_off))
    return points


def matching(cycle_offsets, points):
    table_rows = jnp.asarray(np.array([p[0] for p in points], dtype=np.int32))
    table_cols = jnp.asarray(np.array([p[1] for p in points], dtype=np.int32))
    same = (table_rows[:, None] == cycle_offsets[None, :, 0]) & (
        table_cols[:, None] == cycle_offsets[None, :, 1]
    )
    return same.astype(jnp.int32)


def tile_split(count, rows, cols):
    b = 1
    while b * 2 <= count and cols // (b * 2) >= 128 and count % (b * 2) == 0:
        b *= 2
    a = count // b
    return a, b


def tile_compute(rt, wt, order, place, points, h, w, frames_all, cycle):
    ordered_weight = jnp.take(wt, order, axis=0)
    background = jnp.zeros((rt.shape[0], h, w), jnp.float32)
    for index, (dy, dx) in enumerate(points):
        window = rt[:, HALO + dy : HALO + dy + h, HALO + dx : HALO + dx + w]
        background = background + ordered_weight[index][None] * window
    error = lax.optimization_barrier(rt[:, HALO : HALO + h, HALO : HALO + w] - background)
    grads = jnp.stack(
        [
            jnp.sum(error * rt[:, HALO + dy : HALO + dy + h, HALO + dx : HALO + dx + w], axis=0)
            for dy, dx in points
        ]
    )
    squares = jnp.sum(rt * rt, axis=0)
    energy_sum = jnp.zeros((h, w), jnp.float32)
    for dy, dx in points:
        energy_sum = energy_sum + squares[HALO + dy : HALO + dy + h, HALO + dx : HALO + dx + w]
    gradient = jnp.take(grads, place, axis=0)
    energy = energy_sum / (cycle * frames_all) + 1e-06
    new_weight = wt + gradient / (frames_all * energy)[None]
    return error, new_weight


def exchange_kernel(n, x_ref, o_ref, send_sem, recv_sem, local_sem):
    me = lax.axis_index("tm")
    row = lax.axis_index("rows")
    mesh_id = pl.DeviceIdType.MESH
    barrier = pltpu.get_barrier_semaphore()
    for step in range(1, n):
        peer = lax.rem(me + step, n)
        pl.semaphore_signal(barrier, inc=1, device_id=(row, peer), device_id_type=mesh_id)
    pl.semaphore_wait(barrier, n - 1)
    local = pltpu.make_async_copy(x_ref.at[me], o_ref.at[me], local_sem)
    local.start()
    copies = []
    for step in range(1, n):
        peer = lax.rem(me + step, n)
        copy = pltpu.make_async_remote_copy(
            src_ref=x_ref.at[peer],
            dst_ref=o_ref.at[me],
            send_sem=send_sem.at[step],
            recv_sem=recv_sem.at[step],
            device_id=(row, peer),
            device_id_type=mesh_id,
        )
        copy.start()
        copies.append(copy)
    for copy in copies:
        copy.wait()
    local.wait()


def exchange(x, n, tag):
    anywhere = pl.BlockSpec(memory_space=pl.ANY)
    return pl.pallas_call(
        functools.partial(exchange_kernel, n),
        out_shape=jax.ShapeDtypeStruct(x.shape, x.dtype),
        in_specs=[anywhere],
        out_specs=anywhere,
        scratch_shapes=[
            pltpu.SemaphoreType.DMA((n,)),
            pltpu.SemaphoreType.DMA((n,)),
            pltpu.SemaphoreType.DMA,
        ],
        compiler_params=pltpu.CompilerParams(collective_id=tag, has_side_effects=True),
        name=f"exchange_{tag}",
    )(x)


def return_kernel(n, b, nw_ref, er_ref, nw_out, er_out, send_sem, recv_sem, local_sem):
    me = lax.axis_index("tm")
    row = lax.axis_index("rows")
    mesh_id = pl.DeviceIdType.MESH
    h, w = nw_ref.shape[2], nw_ref.shape[3]
    rows_at = pl.ds(pl.multiple_of((me // b) * h, h), h)
    cols_at = pl.ds(pl.multiple_of((me % b) * w, w), w)
    barrier = pltpu.get_barrier_semaphore()
    for step in range(1, n):
        pl.semaphore_signal(
            barrier, inc=1, device_id=(row, lax.rem(me + step, n)), device_id_type=mesh_id
        )
    pl.semaphore_wait(barrier, n - 1)
    pairs = ((nw_ref, nw_out), (er_ref, er_out))
    local = []
    for which, (src, dst) in enumerate(pairs):
        copy = pltpu.make_async_copy(src.at[me], dst.at[:, rows_at, cols_at], local_sem.at[which])
        copy.start()
        local.append(copy)
    copies = []
    for step in range(1, n):
        peer = lax.rem(me + step, n)
        for which, (src, dst) in enumerate(pairs):
            copy = pltpu.make_async_remote_copy(
                src_ref=src.at[peer],
                dst_ref=dst.at[:, rows_at, cols_at],
                send_sem=send_sem.at[which, step],
                recv_sem=recv_sem.at[which, step],
                device_id=(row, peer),
                device_id_type=mesh_id,
            )
            copy.start()
            copies.append(copy)
    for copy in copies:
        copy.wait()
    for copy in local:
        copy.wait()


def return_exchange(new_t, error_t, n, b, rows_dev, cols, tag):
    anywhere = pl.BlockSpec(memory_space=pl.ANY)
    k_dev, f_dev = new_t.shape[1], error_t.shape[1]
    return pl.pallas_call(
        functools.partial(return_kernel, n, b),
        out_shape=(
            jax.ShapeDtypeStruct((k_dev, rows_dev, cols), new_t.dtype),
            jax.ShapeDtypeStruct((f_dev, rows_dev, cols), error_t.dtype),
        ),
        in_specs=[anywhere, anywhere],
        out_specs=(anywhere, anywhere),
        scratch_shapes=[
            pltpu.SemaphoreType.DMA((2, n)),
            pltpu.SemaphoreType.DMA((2, n)),
            pltpu.SemaphoreType.DMA((2,)),
        ],
        compiler_params=pltpu.CompilerParams(collective_id=tag, has_side_effects=True),
        name=f"exchange_{tag}",
    )(new_t, error_t)


def on_device(residual, cycle_weight, cycle_offsets):
    frames_dev, rows_dev, cols = residual.shape
    k_dev = cycle_weight.shape[0]
    cycle = cycle_offsets.shape[0]
    n = lax.axis_size("tm")
    frames_all = frames_dev * n
    points = cycle_points()
    same = matching(cycle_offsets, points)
    ks = jnp.arange(cycle, dtype=jnp.int32)
    order = jnp.sum(same * ks[None, :], axis=1)
    place = jnp.sum(same * ks[:, None], axis=0)

    a, b = tile_split(n, rows_dev, cols)
    h, w = rows_dev // a, cols // b

    padded = jnp.pad(residual, ((0, 0), (0, 0), (HALO, HALO)))
    ww = w + 2 * HALO
    lanes = 128
    spare = ww - lanes
    tiles = [(i, j) for i in range(a) for j in range(b)]
    main = jnp.stack([padded[:, i * h : (i + 1) * h, j * w : j * w + lanes] for i, j in tiles])
    rest = jnp.stack(
        [padded[:, i * h : (i + 1) * h, j * w + lanes : j * w + ww] for i, j in tiles]
    )
    w_tiles = cycle_weight.reshape(k_dev, a, h, b, w).transpose(1, 3, 0, 2, 4)
    main_rows = frames_dev * h
    w_rows = k_dev * h
    rest_len = frames_dev * h * spare
    rest_rows = -(-rest_len // lanes)
    used = main_rows + w_rows + rest_rows
    total = -(-used // 8) * 8
    send = jnp.concatenate(
        [
            main.reshape(n, main_rows, lanes),
            w_tiles.reshape(n, w_rows, lanes),
            jnp.pad(rest.reshape(n, rest_len), ((0, 0), (0, rest_rows * lanes - rest_len))).reshape(
                n, rest_rows, lanes
            ),
            jnp.zeros((n, total - used, lanes), jnp.float32),
        ],
        axis=1,
    )
    got = exchange(send, n, 0)
    core_main = got[:, :main_rows].reshape(frames_all, h, lanes)
    wt = got[:, main_rows : main_rows + w_rows].reshape(cycle, h, w)
    core_rest = got[:, main_rows + w_rows : used].reshape(n, rest_rows * lanes)[:, :rest_len]
    core = jnp.concatenate([core_main, core_rest.reshape(frames_all, h, spare)], axis=2)

    bands = lax.axis_size("rows")
    down, up = [], []
    for r in range(bands):
        for m in range(n):
            i, j = m // b, m % b
            if i < a - 1:
                down.append((r * n + m, r * n + m + b))
            elif r < bands - 1:
                down.append((r * n + m, (r + 1) * n + j))
            if i > 0:
                up.append((r * n + m, r * n + m - b))
            elif r > 0:
                up.append((r * n + m, (r - 1) * n + (a - 1) * b + j))
    edge_len = frames_all * HALO * ww
    edge_rows = -(-edge_len // 1024) * 8

    def dense(x):
        x = jnp.pad(x.reshape(edge_len), (0, edge_rows * lanes - edge_len))
        return x.reshape(edge_rows, lanes)

    def undense(x):
        return x.reshape(edge_rows * lanes)[:edge_len].reshape(frames_all, HALO, ww)

    above = undense(lax.ppermute(dense(core[:, h - HALO :]), ("rows", "tm"), down))
    below = undense(lax.ppermute(dense(core[:, :HALO]), ("rows", "tm"), up))
    rt = lax.optimization_barrier(jnp.concatenate([above, core, below], axis=1))

    error_t, new_t = tile_compute(rt, wt, order, place, points, h, w, frames_all, cycle)

    return return_exchange(
        new_t.reshape(n, k_dev, h, w), error_t.reshape(n, frames_dev, h, w), n, b, rows_dev, cols, 1
    )


def solution(mesh):
    in_specs = (P("tm", "rows", None), P("tm", "rows", None), P())
    out_specs = (P("tm", "rows", None), P("tm", "rows", None))
    return jax.shard_map(
        on_device, mesh=mesh, in_specs=in_specs, out_specs=out_specs, check_vma=False
    )
```
